256 devices in a mesh: win: 32 (over y, x, core), grp: 8 (over z).
Axes of the slice: x: 4, y: 4, z: 8, core: 2. Of those that a mesh axis runs over, the one named last changes fastest.
Arguments:
- traces: bfloat16 [256, 512, 2048], P(('win', 'grp'))
- pair_lists: int32 [32, 3], P('win'), may hold values from -1 to 3, as said below
- observed: float32 [32, 3, 16, 16, 2048], P('win'), may hold values from -4 to 4
Outputs:
- correl: float32 [32, 3, 16, 16, 2048], P('win', None, None, None, 'grp')
- trace_gradient: bfloat16 [256, 512, 2048], P(('win', 'grp'))
The draws below stay inside these ranges and needn't reach their ends.
Inputs may be any that keep to these rules, and one draw needn't show every extreme that they name: `pair_lists`: each row lists distinct offsets in increasing order, followed by -1 in its empty slots; block a lists only offsets o with a + o < 32; every block lists at least one offset, and block 0 fills all 3 slots and lists offset 4 - 1.
All inputs are finite; a program needn't handle non-finite values.
Results may differ from the reference program's by a relative error of at most 0.014.
Values may be sent and summed in bfloat16 or wider, within the bound.
No kernel may reach another device: no remote copies, remote signals or barrier semaphores. Data moves between devices by JAX's collectives and lax.ppermute only.
A program may use at most 192 MiB of HBM per device.

```python
import math
import jax
import jax.numpy as jnp
from jax import lax

SEG = 2048
FREQ = 1024
BAND = 64
CB = 16
OFFSETS = 4
SLOTS = 3
NB = 32
CH = 512
WINS = 256


def draw_traces(key, part):
    common = jax.random.normal(jax.random.fold_in(key, 11), (WINS, 1, SEG), jnp.float32)
    private = jax.random.normal(jax.random.fold_in(key, 12), (WINS, CH, SEG), jnp.float32)
    channel_scale = jnp.exp(jax.random.uniform(jax.random.fold_in(key, 14), (1, CH, 1), jnp.float32, 0.0, math.log(10.0)))
    coupling = jax.random.uniform(jax.random.fold_in(key, 13), (1, CH, 1), jnp.float32, -1.5, 1.5)
    window_scale = jnp.exp(jax.random.uniform(jax.random.fold_in(key, 15), (WINS, 1, 1), jnp.float32, math.log(0.5), math.log(2.0)))
    return (channel_scale * window_scale * (coupling * common + private)).astype(jnp.bfloat16)


def draw_pair_lists(key, part):
    blocks_col = jnp.arange(NB, dtype=jnp.int32)[:, None]
    offset_row = jnp.arange(OFFSETS, dtype=jnp.int32)[None, :]
    ceiling = 1 << 30
    scores = jax.random.randint(jax.random.fold_in(key, 21), (NB, OFFSETS), 0, 1 << 20, dtype=jnp.int32) * OFFSETS + offset_row
    scores = jnp.where(jnp.logical_and(blocks_col == 0, offset_row == OFFSETS - 1), -1, scores)
    scores = jnp.where(blocks_col + offset_row < NB, scores, ceiling)
    ranking = jnp.argsort(scores, axis=1, stable=True).astype(jnp.int32)
    ranked = jnp.take_along_axis(scores, ranking, axis=1)
    counts = jax.random.randint(jax.random.fold_in(key, 22), (NB, 1), 1, SLOTS + 1, dtype=jnp.int32)
    counts = jnp.where(blocks_col == 0, SLOTS, counts)
    slot_row = jnp.arange(SLOTS, dtype=jnp.int32)[None, :]
    kept_slots = jnp.logical_and(slot_row < counts, ranked[:, :SLOTS] < ceiling)
    chosen = jnp.where(kept_slots, ranking[:, :SLOTS], OFFSETS + 5)
    chosen = jnp.sort(chosen, axis=1)
    return jnp.where(chosen >= OFFSETS, -1, chosen).astype(jnp.int32)


def shard_levels(key, shape, shards, low, high):
    def one(dim, blocks):
        draws = jax.random.uniform(jax.random.fold_in(jax.random.fold_in(key, 6), dim), (blocks,), jnp.float32, low / len(shards), high / len(shards))
        return jnp.repeat(jnp.exp(draws), shape[dim] // blocks).reshape((-1,) + (1,) * (len(shape) - dim - 1))

    factor_of = one(*shards[0])
    for cut in shards[1:]:
        factor_of = factor_of * one(*cut)
    return factor_of


def gaussian(own_key, shape, width, limit, pieces=(), kind=jnp.bfloat16):
    gain = shard_levels(own_key, shape, pieces, -0.22, 0.18) if pieces else 1.0
    values = jax.random.normal(own_key, shape, jnp.float32) * width * gain
    return jnp.minimum(jnp.maximum(values, -limit), limit).astype(kind)


def setup_inputs(seed: int = 0) -> dict:
    splits = jax.random.split(jax.random.key(seed), 4)
    traces = draw_traces(jax.random.fold_in(splits[3], 71), 0)
    pair_lists = draw_pair_lists(jax.random.fold_in(splits[3], 71), 0)
    observed = gaussian(splits[2], (NB, SLOTS, CB, CB, 2 * FREQ), 0.3, 4.0, ((0, 32),), jnp.float32)
    return {"traces": traces, "pair_lists": pair_lists, "observed": observed}


def dft_table(first_column, column_count):
    samples = jnp.arange(SEG, dtype=jnp.int32)
    columns = first_column + jnp.arange(column_count, dtype=jnp.int32)
    harmonic = columns % FREQ
    phases = samples[:, None] * harmonic[None, :] % SEG
    angles = phases.astype(jnp.float32) * (2.0 * math.pi / SEG)
    values = jnp.where(columns[None, :] < FREQ, jnp.cos(angles), -jnp.sin(angles))
    return values.astype(jnp.bfloat16)

def whiten(spectrum):
    halfway = spectrum.shape[-1] // 2
    real_part = spectrum[..., :halfway]
    imag_part = spectrum[..., halfway:]
    power_bins = real_part * real_part + imag_part * imag_part
    banded = power_bins.reshape(power_bins.shape[:-1] + (halfway // BAND, BAND))
    inverse = lax.rsqrt(lax.optimization_barrier(jnp.mean(banded, axis=-1)) + 1e-05)
    spread = jnp.broadcast_to(inverse[..., None], banded.shape).reshape(power_bins.shape)
    return spectrum * jnp.concatenate([spread, spread], axis=-1)

def split_halves(operand):
    halfway = operand.shape[-1] // 2
    return (operand[..., :halfway].astype(jnp.float32), operand[..., halfway:].astype(jnp.float32))

def correlate(leading, trailing):
    lead_real, lead_imag = split_halves(leading)
    trail_real, trail_imag = split_halves(trailing)
    real_sum = jnp.einsum('wif,wjf->ijf', lead_real, trail_real) + jnp.einsum('wif,wjf->ijf', lead_imag, trail_imag)
    imag_sum = jnp.einsum('wif,wjf->ijf', lead_real, trail_imag) - jnp.einsum('wif,wjf->ijf', lead_imag, trail_real)
    return jnp.concatenate([real_sum, imag_sum], axis=-1) / WINS

def pull_first(residual, trailing):
    resid_real, resid_imag = split_halves(residual)
    trail_real, trail_imag = split_halves(trailing)
    real_part = jnp.einsum('ijf,wjf->wif', resid_real, trail_real) + jnp.einsum('ijf,wjf->wif', resid_imag, trail_imag)
    imag_part = jnp.einsum('ijf,wjf->wif', resid_real, trail_imag) - jnp.einsum('ijf,wjf->wif', resid_imag, trail_real)
    return jnp.concatenate([real_part, imag_part], axis=-1)

def pull_second(residual, leading):
    resid_real, resid_imag = split_halves(residual)
    lead_real, lead_imag = split_halves(leading)
    real_part = jnp.einsum('ijf,wif->wjf', resid_real, lead_real) - jnp.einsum('ijf,wif->wjf', resid_imag, lead_imag)
    imag_part = jnp.einsum('ijf,wif->wjf', resid_real, lead_imag) + jnp.einsum('ijf,wif->wjf', resid_imag, lead_real)
    return jnp.concatenate([real_part, imag_part], axis=-1)

def reference(traces, pair_lists, observed):
    dft_matrix = dft_table(0, 2 * FREQ)
    spectra = jnp.dot(traces.reshape(WINS * CH, SEG), dft_matrix, preferred_element_type=jnp.float32)
    spectra = spectra.reshape(WINS, CH, 2 * FREQ)
    whitened = whiten(spectra).astype(jnp.bfloat16)
    blocks = whitened.reshape(WINS, NB, CB, 2 * FREQ)
    live_slots = (pair_lists >= 0).astype(jnp.float32)[:, :, None, None, None]
    partner = jnp.clip(jnp.arange(NB, dtype=jnp.int32)[:, None] + jnp.maximum(pair_lists, 0), 0, NB - 1).astype(jnp.int32)

    def block_of(block_index):
        return lax.dynamic_index_in_dim(blocks, block_index, 1, keepdims=False)

    def stack_block(block_index):
        leading = block_of(block_index)
        return jnp.stack([correlate(leading, block_of(partner[block_index, slot_index])) for slot_index in range(SLOTS)])
    indices = jnp.arange(NB, dtype=jnp.int32)
    correl = lax.map(stack_block, indices) * live_slots
    residual = ((correl - observed) * live_slots).astype(jnp.bfloat16)

    def gradient_block(block_index):
        accum_grad = jnp.zeros((WINS, CB, 2 * FREQ), jnp.float32)
        for slot_index in range(SLOTS):
            accum_grad = accum_grad + pull_first(residual[block_index, slot_index], block_of(partner[block_index, slot_index]))
        for offset in range(OFFSETS):
            source = jnp.maximum(block_index - offset, 0).astype(jnp.int32)
            reached = block_index - offset >= 0
            chosen = jnp.zeros((CB, CB, 2 * FREQ), jnp.bfloat16)
            for slot_index in range(SLOTS):
                matched = jnp.logical_and(reached, pair_lists[source, slot_index] == offset)
                chosen = jnp.where(matched, residual[source, slot_index], chosen)
            accum_grad = accum_grad + pull_second(chosen, block_of(source))
        return accum_grad
    white_grad = lax.map(gradient_block, indices)
    white_grad = jnp.transpose(white_grad, (1, 0, 2, 3)).reshape(WINS, CH, 2 * FREQ).astype(jnp.bfloat16)
    unused, pullback = jax.vjp(whiten, spectra)
    spectra_grad = pullback(white_grad.astype(jnp.float32))[0].astype(jnp.bfloat16)
    trace_gradient = jnp.dot(spectra_grad.reshape(WINS * CH, 2 * FREQ), dft_matrix.T, preferred_element_type=jnp.float32)
    return (correl, trace_gradient.reshape(WINS, CH, SEG).astype(jnp.bfloat16))
```

```python
import functools
import math

import jax
import jax.numpy as jnp
import numpy as np
from jax import lax
from jax.experimental import pallas as pl
from jax.experimental.pallas import tpu as pltpu
from jax.sharding import PartitionSpec as P

SEG = 2048
FREQ = 1024
BAND = 64
OFFSETS = 4
CB = 16
SLOTS = 3
CH = 512
WINS = 256
NB = 32
GRP = 8
KB = 4
LANES = 128
HALF = 64
EMPTY = 64.0
VMEM_LIMIT = 56 << 20

F32 = jnp.float32
BF16 = jnp.bfloat16


def plane_of(q, h):
    return (q + 3) % GRP if h == 0 else (q + 7) % GRP


def table_parts():
    row = np.arange(2 * BAND)
    j = (row // 8) * KB + row % KB
    imag = (row % 8) >= KB
    n = np.arange(SEG)
    ang = 2.0 * math.pi * ((n[None, :] * j[:, None]) % SEG) / SEG
    a = np.where(imag[:, None], -np.sin(ang), np.cos(ang))
    b = np.where(imag[:, None], -np.cos(ang), -np.sin(ang))
    band = np.arange(FREQ // BAND)
    bang = 2.0 * math.pi * ((n[None, :] * (BAND * band[:, None])) % SEG) / SEG
    return [np.asarray(v, np.float32) for v in (a, b, np.cos(bang), np.sin(bang))]


def dot(x, y, cx=1, cy=0):
    return lax.dot_general(x, y, (((cx,), (cy,)), ((), ())), preferred_element_type=F32)


def regroup(inverse):
    out = lax.broadcasted_iota(jnp.int32, (256, 256), 0)
    src = lax.broadcasted_iota(jnp.int32, (256, 256), 1)
    if inverse:
        hit = (src % 32) * 8 + src // 32 == out
    else:
        hit = (out % 32) * 8 + out // 32 == src
    return jnp.where(hit, 1.0, 0.0).astype(BF16)


def full(shape):
    return pl.BlockSpec(shape, lambda *i: (0,) * len(shape))


def forward_kernel(x_ref, a_ref, b_ref, c_ref, s_ref, y_ref, r_ref):
    step = pl.program_id(0)
    parts = []
    for wh in range(2):
        band = step * 2 + wh
        c = c_ref[pl.ds(band, 1), :]
        s = s_ref[pl.ds(band, 1), :]
        parts.append((a_ref[...] * c + b_ref[...] * s).astype(BF16))
    table = jnp.concatenate(parts, axis=0)
    spec = dot(table, x_ref[...], 1, 1)
    for wh in range(2):
        rows = spec[wh * 128 : (wh + 1) * 128]
        level = jnp.sum(rows * rows, axis=0, keepdims=True) * (1.0 / BAND) + 1e-05
        inv = lax.rsqrt(level)
        r_ref[0, wh : wh + 1, :] = inv
        y_ref[wh * 16 : (wh + 1) * 16, 0] = (rows * inv).reshape(16, 8, CH).astype(BF16)


def plane_index(step):
    q, h = step // 2, step % 2
    return jnp.where(h == 0, q + 3, (q + 7) % GRP)


def forward(x, consts):
    return pl.pallas_call(
        forward_kernel,
        grid=(8,),
        in_specs=[full((CH, SEG)), full((128, SEG)), full((128, SEG)), full((16, SEG)), full((16, SEG))],
        out_specs=[
            pl.BlockSpec((32, 1, 8, CH), lambda i: (0, plane_index(i), 0, 0)),
            pl.BlockSpec((1, 2, CH), lambda i: (i, 0, 0)),
        ],
        out_shape=[
            jax.ShapeDtypeStruct((32, GRP, 8, CH), BF16),
            jax.ShapeDtypeStruct((8, 2, CH), F32),
        ],
        compiler_params=pltpu.CompilerParams(vmem_limit_bytes=VMEM_LIMIT),
        cost_estimate=pl.CostEstimate(flops=2 * CH * SEG * SEG, bytes_accessed=8 << 20, transcendentals=0),
        name="forward",
    )(x, *consts)


def backward_kernel(g_ref, y_ref, r_ref, a_ref, b_ref, c_ref, s_ref, o_ref, d_ref):
    @pl.when(pl.program_id(0) == 0)
    def _():
        for step in range(8):
            plane = plane_of(step // 2, step % 2)
            for wh in range(2):
                g = g_ref[wh * 16 : (wh + 1) * 16, plane].astype(F32).reshape(128, CH)
                y = y_ref[wh * 16 : (wh + 1) * 16, plane].astype(F32).reshape(128, CH)
                mean = jnp.sum(g * y, axis=0, keepdims=True) * (1.0 / BAND)
                d = (g - y * mean) * r_ref[step, wh : wh + 1, :]
                row = (step * 2 + wh) * 128
                d_ref[:, row : row + 128] = d.T.astype(BF16)

    parts = []
    for band in range(16):
        c = c_ref[band : band + 1, :]
        s = s_ref[band : band + 1, :]
        parts.append((a_ref[...] * c + b_ref[...] * s).astype(BF16))
    table = jnp.concatenate(parts, axis=0)
    o_ref[...] = dot(d_ref[...], table).astype(BF16)


def backward(g, y, r, consts):
    tile = 256
    col = lambda rows: pl.BlockSpec((rows, tile), lambda i: (0, i))
    return pl.pallas_call(
        backward_kernel,
        grid=(SEG // tile,),
        in_specs=[
            full((32, GRP, 8, CH)),
            full((32, GRP, 8, CH)),
            full((8, 2, CH)),
            col(128),
            col(128),
            col(16),
            col(16),
        ],
        out_specs=pl.BlockSpec((CH, tile), lambda i: (0, i)),
        out_shape=jax.ShapeDtypeStruct((CH, SEG), BF16),
        scratch_shapes=[pltpu.VMEM((CH, SEG), BF16)],
        compiler_params=pltpu.CompilerParams(vmem_limit_bytes=VMEM_LIMIT),
        cost_estimate=pl.CostEstimate(flops=2 * CH * SEG * SEG, bytes_accessed=10 << 20, transcendentals=0),
        name="backward",
    )(g, y, r, *consts)


def pack_kernel(sc_ref, re_ref, im_ref, o_ref):
    perm = regroup(True)
    for ri, src in enumerate((re_ref, im_ref)):
        turned = []
        for i in range(8):
            rows = []
            for ih in range(2):
                for o in range(OFFSETS):
                    val = jnp.full((CB, LANES), EMPTY, F32)
                    for s in range(SLOTS):
                        val = jnp.where(sc_ref[s] == o, src[s, ih * 8 + i], val)
                    rows.append(val)
            turned.append(jnp.concatenate(rows, axis=0).T.astype(BF16))
        for gr in range(4):
            stack = jnp.concatenate([t[gr * 32 : (gr + 1) * 32] for t in turned], axis=0)
            tile = dot(perm, stack).reshape(8, KB, 8, LANES)
            o_ref[gr * 8 : (gr + 1) * 8, ri] = tile.astype(BF16)


def pack_observed(scalars, observed):
    spec = lambda base: pl.BlockSpec((SLOTS, CB, CB, LANES), lambda i, sc: (0, 0, 0, base + sc[3]))
    return pl.pallas_call(
        pack_kernel,
        grid_spec=pltpu.PrefetchScalarGridSpec(
            num_scalar_prefetch=1,
            grid=(1,),
            in_specs=[spec(0), spec(8)],
            out_specs=pl.BlockSpec((32, 2, KB, 8, LANES), lambda i, sc: (0, 0, 0, 0, 0)),
        ),
        out_shape=jax.ShapeDtypeStruct((32, 2, KB, 8, LANES), BF16),
        compiler_params=pltpu.CompilerParams(vmem_limit_bytes=VMEM_LIMIT),
        name="pack_observed",
    )(scalars, observed, observed)


def middle_kernel(sc_ref, x_ref, obs_ref, corr_ref, out_ref, u_ref, d_ref):
    half = sc_ref[4]
    perm = regroup(False)
    for gr in range(8):
        y = dot(perm, x_ref[gr * 256 : (gr + 1) * 256, :]).astype(BF16)
        for r8 in range(8):
            ri, k = r8 // KB, r8 % KB
            row = ri * WINS + gr * 32
            u_ref[k, row : row + 32, :] = y[r8 * 32 : (r8 + 1) * 32]

    lane8 = lax.broadcasted_iota(jnp.int32, (8, LANES), 1)
    lane16 = lax.broadcasted_iota(jnp.int32, (16, LANES), 1)

    def one_bin(k, carry):
        later = None
        for b in range(4):
            width = 2 if b < 3 else 1
            cols = slice(b * LANES, (b + width) * LANES)
            lead = u_ref[k, :, b * LANES : (b + 1) * LANES]
            re_rows = u_ref[k, :WINS, cols]
            im_rows = u_ref[k, WINS:, cols]
            straight = jnp.concatenate([re_rows, im_rows], axis=0)
            crossed = jnp.concatenate([im_rows, -re_rows], axis=0)
            gram = dot(lead.T, jnp.concatenate([straight, crossed], axis=1))
            tiles = ([], [])
            for blk in range(8):
                a, shift = b * 8 + blk, blk * CB
                for ri in range(2):
                    base = ri * width * LANES
                    here = gram[shift : shift + 16, base : base + LANES]
                    if shift > 0:
                        if shift > HALF and width == 2:
                            there = gram[shift : shift + 16, base + LANES : base + 2 * LANES]
                            here = jnp.where(lane16 >= shift, here, there)
                        here = pltpu.roll(here, LANES - shift, 1)
                    packed = jnp.where(lane8 < HALF, here[:8], pltpu.roll(here[8:], HALF, 1))
                    packed = packed * (1.0 / WINS)
                    seen = obs_ref[a, ri, k].astype(F32)
                    live = seen < EMPTY / 2
                    slot = 1 - half if ri == 0 else half
                    corr_ref[slot, a, k] = packed.astype(BF16)
                    resid = jnp.where(live, packed - seen, 0.0)
                    spread = jnp.concatenate([resid, pltpu.roll(resid, HALF, 1)], axis=0)
                    spread = jnp.where(lane16 < HALF, spread, 0.0)
                    if shift > 0:
                        spread = pltpu.roll(spread, shift, 1)
                    if shift > HALF:
                        first = jnp.where(lane16 >= shift, spread, 0.0)
                        second = jnp.where(lane16 < shift, spread, 0.0)
                    else:
                        first, second = spread, jnp.zeros_like(spread)
                    tiles[ri].append([first, second][:width])
            res = [
                [jnp.concatenate([t[p] for t in tiles[ri]], axis=0).astype(BF16) for p in range(width)]
                for ri in range(2)
            ]
            top = jnp.concatenate([m for p in range(width) for m in (res[0][p], res[1][p])], axis=1)
            low = jnp.concatenate([m for p in range(width) for m in (-res[1][p], res[0][p])], axis=1)
            weights = jnp.concatenate([top, low], axis=0)
            waves = [
                u_ref[k, ri * WINS : (ri + 1) * WINS, (b + p) * LANES : (b + p + 1) * LANES]
                for p in range(width)
                for ri in range(2)
            ]
            pulled = dot(jnp.concatenate(waves, axis=1), weights, 1, 1)
            pushed = dot(jnp.concatenate(waves[:2], axis=1), weights)
            grad = pulled + pushed[:, :256]
            if later is not None:
                grad = grad + later
            later = pushed[:, 256:] if width == 2 else None
            d_ref[k, :WINS, b * LANES : (b + 1) * LANES] = grad[:, :LANES].astype(BF16)
            d_ref[k, WINS:, b * LANES : (b + 1) * LANES] = grad[:, LANES:].astype(BF16)
        return carry

    lax.fori_loop(0, KB, one_bin, 0)
    back = regroup(True)
    for gr in range(8):
        rows = jnp.concatenate(
            [
                d_ref[r8 % KB, (r8 // KB) * WINS + gr * 32 : (r8 // KB) * WINS + gr * 32 + 32, :]
                for r8 in range(8)
            ],
            axis=0,
        )
        out_ref[gr * 256 : (gr + 1) * 256, :] = dot(back, rows).astype(BF16)


def middle(scalars, x, obs):
    block = lambda shape: pl.BlockSpec(shape, lambda i, sc: (0,) * len(shape))
    return pl.pallas_call(
        middle_kernel,
        grid_spec=pltpu.PrefetchScalarGridSpec(
            num_scalar_prefetch=1,
            grid=(1,),
            in_specs=[block((2048, CH)), block((NB, 2, KB, 8, LANES))],
            out_specs=[block((2, NB, KB, 8, LANES)), block((2048, CH))],
            scratch_shapes=[pltpu.VMEM((KB, 2 * WINS, CH), BF16), pltpu.VMEM((KB, 2 * WINS, CH), BF16)],
        ),
        out_shape=[
            jax.ShapeDtypeStruct((2, NB, KB, 8, LANES), BF16),
            jax.ShapeDtypeStruct((2048, CH), BF16),
        ],
        compiler_params=pltpu.CompilerParams(vmem_limit_bytes=VMEM_LIMIT),
        name="middle",
    )(scalars, x, obs)


def unpack_kernel(sc_ref, x_ref, o_ref):
    perm = regroup(False)
    for h in range(2):
        first = sc_ref[5]
        index = first if h == 0 else 1 - first
        regrouped = []
        for gr in range(4):
            rows = x_ref[gr * 8 : (gr + 1) * 8, index].astype(F32).reshape(256, LANES).astype(BF16)
            regrouped.append(dot(perm, rows))
        for i in range(8):
            page = jnp.concatenate([r[i * 32 : (i + 1) * 32] for r in regrouped], axis=0)
            turned = page.T
            for ih in range(2):
                for s in range(SLOTS):
                    val = jnp.zeros((CB, LANES), F32)
                    for o in range(OFFSETS):
                        row = ih * HALF + o * CB
                        val = jnp.where(sc_ref[s] == o, turned[row : row + CB], val)
                    o_ref[s, ih * 8 + i, :, h * LANES : (h + 1) * LANES] = val


def unpack_correl(scalars, x):
    block = lambda shape: pl.BlockSpec(shape, lambda i, sc: (0,) * len(shape))
    return pl.pallas_call(
        unpack_kernel,
        grid_spec=pltpu.PrefetchScalarGridSpec(
            num_scalar_prefetch=1,
            grid=(1,),
            in_specs=[block((32, 2, KB, 8, LANES))],
            out_specs=block((SLOTS, CB, CB, 2 * LANES)),
        ),
        out_shape=jax.ShapeDtypeStruct((SLOTS, CB, CB, 2 * LANES), F32),
        compiler_params=pltpu.CompilerParams(vmem_limit_bytes=VMEM_LIMIT),
        name="unpack_correl",
    )(scalars, x)


def on_device(traces, pair_lists, observed):
    consts = [jnp.asarray(v) for v in table_parts()]
    g = lax.axis_index("grp")
    half = jnp.where(jnp.logical_and(g >= 3, g <= 6), 0, 1)
    q = jnp.where(half == 0, g - 3, (g + 1) % GRP)
    low = jnp.where(g < 4, 1, 0)
    scalars = jnp.concatenate([pair_lists[0], jnp.stack([2 * q + half, half, low]).astype(jnp.int32)])

    packed = pack_observed(scalars, observed[0])
    seen = lax.all_to_all(packed, "win", 0, 0)
    white, inverse = forward(traces[0], consts)
    moved = lax.all_to_all(white.reshape(WINS, 8, CH), ("win", "grp"), 0, 0)
    corr, grad = middle(scalars, moved.reshape(2048, CH), seen)
    up = lax.ppermute(corr[0], "grp", [(i, (i + 1) % GRP) for i in range(GRP)])
    down = lax.ppermute(corr[1], "grp", [(i, (i - 3) % GRP) for i in range(GRP)])
    returned = lax.all_to_all(grad.reshape(WINS, 8, CH), ("win", "grp"), 0, 0)
    owned = lax.all_to_all(jnp.stack([up, down], axis=1), "win", 0, 0)
    trace_grad = backward(returned.reshape(32, GRP, 8, CH), white, inverse, consts)
    correl = unpack_correl(scalars, owned)
    return correl[None], trace_grad[None]


def solution(mesh):
    return jax.shard_map(
        on_device,
        mesh=mesh,
        in_specs=(P(("win", "grp"), None, None), P("win", None), P("win", None, None, None, None)),
        out_specs=(P("win", None, None, None, "grp"), P(("win", "grp"), None, None)),
        check_vma=False,
    )
```

```python
import functools
import math

import jax
import jax.numpy as jnp
import numpy as np
from jax import lax
from jax.experimental import pallas as pl
from jax.experimental.pallas import tpu as pltpu
from jax.sharding import PartitionSpec as P

SEG = 2048
FREQ = 1024
BAND = 64
OFFSETS = 4
CB = 16
SLOTS = 3
CH = 512
WINS = 256
NB = 32
GRP = 8
KB = 4
LANES = 128
HALF = 64
EMPTY = 64.0
VMEM_LIMIT = 56 << 20

F32 = jnp.float32
BF16 = jnp.bfloat16


def plane_of(q, h):
    return (q + 3) % GRP if h == 0 else (q + 7) % GRP


def table_parts():
    row = np.arange(2 * BAND)
    j = (row // 8) * KB + row % KB
    imag = (row % 8) >= KB
    n = np.arange(SEG)
    ang = 2.0 * math.pi * ((n[None, :] * j[:, None]) % SEG) / SEG
    a = np.where(imag[:, None], -np.sin(ang), np.cos(ang))
    b = np.where(imag[:, None], -np.cos(ang), -np.sin(ang))
    band = np.arange(FREQ // BAND)
    bang = 2.0 * math.pi * ((n[None, :] * (BAND * band[:, None])) % SEG) / SEG
    return [np.asarray(v, np.float32) for v in (a, b, np.cos(bang), np.sin(bang))]


def dot(x, y, cx=1, cy=0):
    return lax.dot_general(x, y, (((cx,), (cy,)), ((), ())), preferred_element_type=F32)


def regroup(inverse):
    out = lax.broadcasted_iota(jnp.int32, (256, 256), 0)
    src = lax.broadcasted_iota(jnp.int32, (256, 256), 1)
    if inverse:
        hit = (src % 32) * 8 + src // 32 == out
    else:
        hit = (out % 32) * 8 + out // 32 == src
    return jnp.where(hit, 1.0, 0.0).astype(BF16)


def full(shape):
    return pl.BlockSpec(shape, lambda *i: (0,) * len(shape))


def forward_kernel(x_ref, a_ref, b_ref, c_ref, s_ref, y_ref, r_ref):
    step = pl.program_id(0)
    parts = []
    for wh in range(2):
        band = step * 2 + wh
        c = c_ref[pl.ds(band, 1), :]
        s = s_ref[pl.ds(band, 1), :]
        parts.append((a_ref[...] * c + b_ref[...] * s).astype(BF16))
    table = jnp.concatenate(parts, axis=0)
    spec = dot(table, x_ref[...], 1, 1)
    for wh in range(2):
        rows = spec[wh * 128 : (wh + 1) * 128]
        level = jnp.sum(rows * rows, axis=0, keepdims=True) * (1.0 / BAND) + 1e-05
        inv = lax.rsqrt(level)
        r_ref[0, wh : wh + 1, :] = inv
        y_ref[wh * 16 : (wh + 1) * 16, 0] = (rows * inv).reshape(16, 8, CH).astype(BF16)


def plane_index(step):
    q, h = step // 2, step % 2
    return jnp.where(h == 0, q + 3, (q + 7) % GRP)


def forward(x, consts):
    return pl.pallas_call(
        forward_kernel,
        grid=(8,),
        in_specs=[full((CH, SEG)), full((128, SEG)), full((128, SEG)), full((16, SEG)), full((16, SEG))],
        out_specs=[
            pl.BlockSpec((32, 1, 8, CH), lambda i: (0, plane_index(i), 0, 0)),
            pl.BlockSpec((1, 2, CH), lambda i: (i, 0, 0)),
        ],
        out_shape=[
            jax.ShapeDtypeStruct((32, GRP, 8, CH), BF16),
            jax.ShapeDtypeStruct((8, 2, CH), F32),
        ],
        compiler_params=pltpu.CompilerParams(vmem_limit_bytes=VMEM_LIMIT),
        cost_estimate=pl.CostEstimate(flops=2 * CH * SEG * SEG, bytes_accessed=8 << 20, transcendentals=0),
        name="forward",
    )(x, *consts)


def backward_kernel(g_ref, y_ref, r_ref, a_ref, b_ref, c_ref, s_ref, o_ref, d_ref):
    @pl.when(pl.program_id(0) == 0)
    def _():
        for step in range(8):
            plane = plane_of(step // 2, step % 2)
            for wh in range(2):
                g = g_ref[wh * 16 : (wh + 1) * 16, plane].astype(F32).reshape(128, CH)
                y = y_ref[wh * 16 : (wh + 1) * 16, plane].astype(F32).reshape(128, CH)
                mean = jnp.sum(g * y, axis=0, keepdims=True) * (1.0 / BAND)
                d = (g - y * mean) * r_ref[step, wh : wh + 1, :]
                row = (step * 2 + wh) * 128
                d_ref[:, row : row + 128] = d.T.astype(BF16)

    parts = []
    for band in range(16):
        c = c_ref[band : band + 1, :]
        s = s_ref[band : band + 1, :]
        parts.append((a_ref[...] * c + b_ref[...] * s).astype(BF16))
    table = jnp.concatenate(parts, axis=0)
    o_ref[...] = dot(d_ref[...], table).astype(BF16)


def backward(g, y, r, consts):
    tile = 256
    col = lambda rows: pl.BlockSpec((rows, tile), lambda i: (0, i))
    return pl.pallas_call(
        backward_kernel,
        grid=(SEG // tile,),
        in_specs=[
            full((32, GRP, 8, CH)),
            full((32, GRP, 8, CH)),
            full((8, 2, CH)),
            col(128),
            col(128),
            col(16),
            col(16),
        ],
        out_specs=pl.BlockSpec((CH, tile), lambda i: (0, i)),
        out_shape=jax.ShapeDtypeStruct((CH, SEG), BF16),
        scratch_shapes=[pltpu.VMEM((CH, SEG), BF16)],
        compiler_params=pltpu.CompilerParams(vmem_limit_bytes=VMEM_LIMIT),
        cost_estimate=pl.CostEstimate(flops=2 * CH * SEG * SEG, bytes_accessed=10 << 20, transcendentals=0),
        name="backward",
    )(g, y, r, *consts)


def pack_kernel(sc_ref, re_ref, im_ref, o_ref):
    perm = regroup(True)
    for ri, src in enumerate((re_ref, im_ref)):
        turned = []
        for i in range(8):
            rows = []
            for ih in range(2):
                for o in range(OFFSETS):
                    val = jnp.full((CB, LANES), EMPTY, F32)
                    for s in range(SLOTS):
                        val = jnp.where(sc_ref[s] == o, src[s, ih * 8 + i], val)
                    rows.append(val)
            turned.append(jnp.concatenate(rows, axis=0).T.astype(BF16))
        for gr in range(4):
            stack = jnp.concatenate([t[gr * 32 : (gr + 1) * 32] for t in turned], axis=0)
            tile = dot(perm, stack).reshape(8, KB, 8, LANES)
            o_ref[gr * 8 : (gr + 1) * 8, ri] = tile.astype(BF16)


def pack_observed(scalars, observed):
    spec = lambda base: pl.BlockSpec((SLOTS, CB, CB, LANES), lambda i, sc: (0, 0, 0, base + sc[3]))
    return pl.pallas_call(
        pack_kernel,
        grid_spec=pltpu.PrefetchScalarGridSpec(
            num_scalar_prefetch=1,
            grid=(1,),
            in_specs=[spec(0), spec(8)],
            out_specs=pl.BlockSpec((32, 2, KB, 8, LANES), lambda i, sc: (0, 0, 0, 0, 0)),
        ),
        out_shape=jax.ShapeDtypeStruct((32, 2, KB, 8, LANES), BF16),
        compiler_params=pltpu.CompilerParams(vmem_limit_bytes=VMEM_LIMIT),
        name="pack_observed",
    )(scalars, observed, observed)


def middle_kernel(sc_ref, x_ref, obs_ref, corr_ref, out_ref, u_ref, d_ref):
    half = sc_ref[4]
    perm = regroup(False)
    for gr in range(8):
        y = dot(perm, x_ref[gr * 256 : (gr + 1) * 256, :]).astype(BF16)
        for r8 in range(8):
            ri, k = r8 // KB, r8 % KB
            row = ri * WINS + gr * 32
            u_ref[k, row : row + 32, :] = y[r8 * 32 : (r8 + 1) * 32]

    lane8 = lax.broadcasted_iota(jnp.int32, (8, LANES), 1)
    lane16 = lax.broadcasted_iota(jnp.int32, (16, LANES), 1)

    def one_bin(k, carry):
        later = None
        for b in range(4):
            width = 2 if b < 3 else 1
            cols = slice(b * LANES, (b + width) * LANES)
            lead = u_ref[k, :, b * LANES : (b + 1) * LANES]
            re_rows = u_ref[k, :WINS, cols]
            im_rows = u_ref[k, WINS:, cols]
            straight = jnp.concatenate([re_rows, im_rows], axis=0)
            crossed = jnp.concatenate([im_rows, -re_rows], axis=0)
            gram = dot(lead.T, jnp.concatenate([straight, crossed], axis=1))
            tiles = ([], [])
            for blk in range(8):
                a, shift = b * 8 + blk, blk * CB
                for ri in range(2):
                    base = ri * width * LANES
                    here = gram[shift : shift + 16, base : base + LANES]
                    if shift > 0:
                        if shift > HALF and width == 2:
                            there = gram[shift : shift + 16, base + LANES : base + 2 * LANES]
                            here = jnp.where(lane16 >= shift, here, there)
                        here = pltpu.roll(here, LANES - shift, 1)
                    packed = jnp.where(lane8 < HALF, here[:8], pltpu.roll(here[8:], HALF, 1))
                    packed = packed * (1.0 / WINS)
                    seen = obs_ref[a, ri, k].astype(F32)
                    live = seen < EMPTY / 2
                    slot = 1 - half if ri == 0 else half
                    corr_ref[slot, a, k] = packed.astype(BF16)
                    resid = jnp.where(live, packed - seen, 0.0)
                    spread = jnp.concatenate([resid, pltpu.roll(resid, HALF, 1)], axis=0)
                    spread = jnp.where(lane16 < HALF, spread, 0.0)
                    if shift > 0:
                        spread = pltpu.roll(spread, shift, 1)
                    if shift > HALF:
                        first = jnp.where(lane16 >= shift, spread, 0.0)
                        second = jnp.where(lane16 < shift, spread, 0.0)
                    else:
                        first, second = spread, jnp.zeros_like(spread)
                    tiles[ri].append([first, second][:width])
            res = [
                [jnp.concatenate([t[p] for t in tiles[ri]], axis=0).astype(BF16) for p in range(width)]
                for ri in range(2)
            ]
            top = jnp.concatenate([m for p in range(width) for m in (res[0][p], res[1][p])], axis=1)
            low = jnp.concatenate([m for p in range(width) for m in (-res[1][p], res[0][p])], axis=1)
            weights = jnp.concatenate([top, low], axis=0)
            waves = [
                u_ref[k, ri * WINS : (ri + 1) * WINS, (b + p) * LANES : (b + p + 1) * LANES]
                for p in range(width)
                for ri in range(2)
            ]
            pulled = dot(jnp.concatenate(waves, axis=1), weights, 1, 1)
            pushed = dot(jnp.concatenate(waves[:2], axis=1), weights)
            grad = pulled + pushed[:, :256]
            if later is not None:
                grad = grad + later
            later = pushed[:, 256:] if width == 2 else None
            d_ref[k, :WINS, b * LANES : (b + 1) * LANES] = grad[:, :LANES].astype(BF16)
            d_ref[k, WINS:, b * LANES : (b + 1) * LANES] = grad[:, LANES:].astype(BF16)
        return carry

    lax.fori_loop(0, KB, one_bin, 0)
    back = regroup(True)
    for gr in range(8):
        rows = jnp.concatenate(
            [
                d_ref[r8 % KB, (r8 // KB) * WINS + gr * 32 : (r8 // KB) * WINS + gr * 32 + 32, :]
                for r8 in range(8)
            ],
            axis=0,
        )
        out_ref[gr * 256 : (gr + 1) * 256, :] = dot(back, rows).astype(BF16)


def middle(scalars, x, obs):
    block = lambda shape: pl.BlockSpec(shape, lambda i, sc: (0,) * len(shape))
    return pl.pallas_call(
        middle_kernel,
        grid_spec=pltpu.PrefetchScalarGridSpec(
            num_scalar_prefetch=1,
            grid=(1,),
            in_specs=[block((2048, CH)), block((NB, 2, KB, 8, LANES))],
            out_specs=[block((2, NB, KB, 8, LANES)), block((2048, CH))],
            scratch_shapes=[pltpu.VMEM((KB, 2 * WINS, CH), BF16), pltpu.VMEM((KB, 2 * WINS, CH), BF16)],
        ),
        out_shape=[
            jax.ShapeDtypeStruct((2, NB, KB, 8, LANES), BF16),
            jax.ShapeDtypeStruct((2048, CH), BF16),
        ],
        compiler_params=pltpu.CompilerParams(vmem_limit_bytes=VMEM_LIMIT),
        name="middle",
    )(scalars, x, obs)


def unpack_kernel(sc_ref, x_ref, o_ref):
    perm = regroup(False)
    for h in range(2):
        first = sc_ref[5]
        index = first if h == 0 else 1 - first
        regrouped = []
        for gr in range(4):
            rows = x_ref[gr * 8 : (gr + 1) * 8, index].astype(F32).reshape(256, LANES).astype(BF16)
            regrouped.append(dot(perm, rows))
        for i in range(8):
            page = jnp.concatenate([r[i * 32 : (i + 1) * 32] for r in regrouped], axis=0)
            turned = page.T
            for ih in range(2):
                for s in range(SLOTS):
                    val = jnp.zeros((CB, LANES), F32)
                    for o in range(OFFSETS):
                        row = ih * HALF + o * CB
                        val = jnp.where(sc_ref[s] == o, turned[row : row + CB], val)
                    o_ref[s, ih * 8 + i, :, h * LANES : (h + 1) * LANES] = val


def unpack_correl(scalars, x):
    block = lambda shape: pl.BlockSpec(shape, lambda i, sc: (0,) * len(shape))
    return pl.pallas_call(
        unpack_kernel,
        grid_spec=pltpu.PrefetchScalarGridSpec(
            num_scalar_prefetch=1,
            grid=(1,),
            in_specs=[block((32, 2, KB, 8, LANES))],
            out_specs=block((SLOTS, CB, CB, 2 * LANES)),
        ),
        out_shape=jax.ShapeDtypeStruct((SLOTS, CB, CB, 2 * LANES), F32),
        compiler_params=pltpu.CompilerParams(vmem_limit_bytes=VMEM_LIMIT),
        name="unpack_correl",
    )(scalars, x)


def on_device(traces, pair_lists, observed):
    consts = [jnp.asarray(v) for v in table_parts()]
    g = lax.axis_index("grp")
    half = jnp.where(jnp.logical_and(g >= 3, g <= 6), 0, 1)
    q = jnp.where(half == 0, g - 3, (g + 1) % GRP)
    low = jnp.where(g < 4, 1, 0)
    scalars = jnp.concatenate([pair_lists[0], jnp.stack([2 * q + half, half, low]).astype(jnp.int32)])

    packed = pack_observed(scalars, observed[0])
    seen = lax.all_to_all(packed, "win", 0, 0)
    white, inverse = forward(traces[0], consts)
    moved = lax.all_to_all(white.reshape(WINS, 8, CH), ("win", "grp"), 0, 0)
    corr, grad = middle(scalars, moved.reshape(2048, CH), seen)
    up = lax.ppermute(corr[0], "grp", [(i, (i + 1) % GRP) for i in range(GRP)])
    down = lax.ppermute(corr[1], "grp", [(i, (i - 3) % GRP) for i in range(GRP)])
    returned = lax.all_to_all(grad.reshape(WINS, 8, CH), ("win", "grp"), 0, 0)
    up, down, returned = lax.optimization_barrier((up, down, returned))
    owned = lax.all_to_all(jnp.stack([up, down], axis=1), "win", 0, 0)
    trace_grad = backward(returned.reshape(32, GRP, 8, CH), white, inverse, consts)
    correl = unpack_correl(scalars, owned)
    return correl[None], trace_grad[None]


def solution(mesh):
    return jax.shard_map(
        on_device,
        mesh=mesh,
        in_specs=(P(("win", "grp"), None, None), P("win", None), P("win", None, None, None, None)),
        out_specs=(P("win", None, None, None, "grp"), P(("win", "grp"), None, None)),
        check_vma=False,
    )
```

```python
import functools
import math

import jax
import jax.numpy as jnp
import numpy as np
from jax import lax
from jax.experimental import pallas as pl
from jax.experimental.pallas import tpu as pltpu
from jax.sharding import PartitionSpec as P

SEG = 2048
FREQ = 1024
BAND = 64
OFFSETS = 4
CB = 16
SLOTS = 3
CH = 512
WINS = 256
NB = 32
GRP = 8
KB = 4
LANES = 128
HALF = 64
EMPTY = 64.0
VMEM_LIMIT = 56 << 20

F32 = jnp.float32
BF16 = jnp.bfloat16


def half_of(g):
    return jnp.where(jnp.logical_and(g >= 3, g <= 6), 0, 1)


def quarter_of(g):
    return jnp.where(half_of(g) == 0, g - 3, (g + 1) % GRP)


def table_parts():
    row = np.arange(2 * BAND)
    j = (row % 64) // 8 * 8 + row % KB * 2 + row // 64
    imag = (row % 8) >= KB
    n = np.arange(SEG // 2)
    ang = 2.0 * math.pi * ((n[None, :] * j[:, None]) % SEG) / SEG
    a = np.where(imag[:, None], -np.sin(ang), np.cos(ang))
    b = np.where(imag[:, None], -np.cos(ang), -np.sin(ang))
    band = np.arange(FREQ // BAND)
    bang = 2.0 * math.pi * ((n[None, :] * (BAND * band[:, None])) % SEG) / SEG
    return [np.asarray(v, np.float32) for v in (a, b, np.cos(bang), np.sin(bang))]


def dot(x, y, cx=1, cy=0):
    return lax.dot_general(x, y, (((cx,), (cy,)), ((), ())), preferred_element_type=F32)


def regroup(inverse, bins=False):
    shape = (256, 256)
    near = lax.broadcasted_iota(jnp.int32, shape, 1 if inverse else 0)
    far = lax.broadcasted_iota(jnp.int32, shape, 0 if inverse else 1)
    c = near % 32
    if bins:
        c = c // 8 * 8 + c % 2 * KB + c % 8 // 2
    return jnp.where(c * 8 + near // 32 == far, 1.0, 0.0).astype(BF16)


def full(shape):
    return pl.BlockSpec(shape, lambda *i: (0,) * len(shape))


def forward_kernel(x_ref, a_ref, b_ref, c_ref, s_ref, y_ref, r_ref, h_ref):
    step = pl.program_id(0)

    @pl.when(step == 0)
    def _():
        early = x_ref[:, : SEG // 2].astype(F32)
        late = x_ref[:, SEG // 2 :].astype(F32)
        h_ref[0] = (early + late).astype(BF16)
        h_ref[1] = (early - late).astype(BF16)

    waves = []
    for p in range(2):
        a = a_ref[p * 64 : (p + 1) * 64]
        b = b_ref[p * 64 : (p + 1) * 64]
        parts = []
        for gi in range(2):
            g = step * 2 + gi
            for wh in range(2):
                band = quarter_of(g) * 4 + half_of(g) * 2 + wh
                parts.append((a * c_ref[pl.ds(band, 1), :] + b * s_ref[pl.ds(band, 1), :]).astype(BF16))
        waves.append(dot(jnp.concatenate(parts, axis=0), h_ref[p], 1, 1))
    for gi in range(2):
        for wh in range(2):
            row = (gi * 2 + wh) * 64
            rows = [w[row : row + 64] for w in waves]
            level = jnp.sum(rows[0] * rows[0] + rows[1] * rows[1], axis=0, keepdims=True)
            inv = lax.rsqrt(level * (1.0 / BAND) + 1e-05)
            r_ref[gi, wh : wh + 1, :] = inv
            for p in range(2):
                y_ref[wh * 8 : (wh + 1) * 8, p, gi] = (rows[p] * inv).reshape(8, 8, CH).astype(BF16)


def forward(x, consts):
    return pl.pallas_call(
        forward_kernel,
        grid=(4,),
        in_specs=[full((CH, SEG)), full((128, SEG // 2)), full((128, SEG // 2)), full((16, SEG // 2)), full((16, SEG // 2))],
        out_specs=[
            pl.BlockSpec((16, 2, 2, 8, CH), lambda i: (0, 0, i, 0, 0)),
            pl.BlockSpec((2, 2, CH), lambda i: (i, 0, 0)),
        ],
        out_shape=[
            jax.ShapeDtypeStruct((16, 2, GRP, 8, CH), BF16),
            jax.ShapeDtypeStruct((GRP, 2, CH), F32),
        ],
        scratch_shapes=[pltpu.VMEM((2, CH, SEG // 2), BF16)],
        compiler_params=pltpu.CompilerParams(vmem_limit_bytes=VMEM_LIMIT),
        cost_estimate=pl.CostEstimate(flops=CH * SEG * SEG, bytes_accessed=8 << 20, transcendentals=0),
        name="forward",
    )(x, *consts)


def backward_kernel(g_ref, y_ref, r_ref, a_ref, b_ref, c_ref, s_ref, o_ref, d_ref, late_ref):
    step = pl.program_id(0)

    @pl.when(step == 0)
    def _():
        for plane in range(GRP):
            sides = ([], [])
            for wh in range(2):
                at = slice(wh * 8, (wh + 1) * 8)
                g = [g_ref[at, p, plane].astype(F32).reshape(64, CH) for p in range(2)]
                y = [y_ref[at, p, plane].astype(F32).reshape(64, CH) for p in range(2)]
                inv = r_ref[plane, wh : wh + 1, :]
                mean = jnp.sum(g[0] * y[0] + g[1] * y[1], axis=0, keepdims=True) * (1.0 / BAND)
                for p in range(2):
                    sides[p].append((g[p] - y[p] * mean) * inv)
            for p in range(2):
                turned = jnp.concatenate(sides[p], axis=0).T
                d_ref[p, :, plane * 128 : (plane + 1) * 128] = turned.astype(BF16)

    @pl.when(step % 2 == 0)
    def _():
        waves = []
        for p in range(2):
            a = a_ref[p * 64 : (p + 1) * 64]
            b = b_ref[p * 64 : (p + 1) * 64]
            parts = []
            for plane in range(GRP):
                h = 0 if 3 <= plane <= 6 else 1
                q = plane - 3 if h == 0 else (plane + 1) % GRP
                for band in (q * 4 + h * 2, q * 4 + h * 2 + 1):
                    parts.append((a * c_ref[band : band + 1, :] + b * s_ref[band : band + 1, :]).astype(BF16))
            waves.append(dot(d_ref[p], jnp.concatenate(parts, axis=0)))
        o_ref[...] = (waves[0] + waves[1]).astype(BF16)
        late_ref[...] = (waves[0] - waves[1]).astype(BF16)

    @pl.when(step % 2 == 1)
    def _():
        o_ref[...] = late_ref[...]


def backward(g, y, r, consts):
    tile = 256
    tiles = SEG // 2 // tile
    col = lambda rows: pl.BlockSpec((rows, tile), lambda i: (0, i // 2))
    return pl.pallas_call(
        backward_kernel,
        grid=(2 * tiles,),
        in_specs=[
            full((16, 2, GRP, 8, CH)),
            full((16, 2, GRP, 8, CH)),
            full((GRP, 2, CH)),
            col(128),
            col(128),
            col(16),
            col(16),
        ],
        out_specs=pl.BlockSpec((CH, tile), lambda i: (0, i // 2 + i % 2 * tiles)),
        out_shape=jax.ShapeDtypeStruct((CH, SEG), BF16),
        scratch_shapes=[pltpu.VMEM((2, CH, SEG // 2), BF16), pltpu.VMEM((CH, tile), BF16)],
        compiler_params=pltpu.CompilerParams(vmem_limit_bytes=VMEM_LIMIT),
        cost_estimate=pl.CostEstimate(flops=CH * SEG * SEG, bytes_accessed=10 << 20, transcendentals=0),
        name="backward",
    )(g, y, r, *consts)


def pack_kernel(sc_ref, re_ref, im_ref, o_ref):
    perm = regroup(True, True)
    for ri, src in enumerate((re_ref, im_ref)):
        turned = []
        for i in range(8):
            rows = []
            for ih in range(2):
                for o in range(OFFSETS):
                    val = jnp.full((CB, LANES), EMPTY, F32)
                    for s in range(SLOTS):
                        val = jnp.where(sc_ref[s] == o, src[s, ih * 8 + i], val)
                    rows.append(val)
            turned.append(jnp.concatenate(rows, axis=0).T.astype(BF16))
        for gr in range(4):
            stack = jnp.concatenate([t[gr * 32 : (gr + 1) * 32] for t in turned], axis=0)
            tile = dot(perm, stack).reshape(8, KB, 8, LANES)
            o_ref[gr * 8 : (gr + 1) * 8, ri] = tile.astype(BF16)


def pack_observed(scalars, observed):
    spec = lambda base: pl.BlockSpec((SLOTS, CB, CB, LANES), lambda i, sc: (0, 0, 0, base + sc[3]))
    return pl.pallas_call(
        pack_kernel,
        grid_spec=pltpu.PrefetchScalarGridSpec(
            num_scalar_prefetch=1,
            grid=(1,),
            in_specs=[spec(0), spec(8)],
            out_specs=pl.BlockSpec((32, 2, KB, 8, LANES), lambda i, sc: (0, 0, 0, 0, 0)),
        ),
        out_shape=jax.ShapeDtypeStruct((32, 2, KB, 8, LANES), BF16),
        compiler_params=pltpu.CompilerParams(vmem_limit_bytes=VMEM_LIMIT),
        name="pack_observed",
    )(scalars, observed, observed)


def middle_kernel(sc_ref, x_ref, obs_ref, corr_ref, out_ref, u_ref, d_ref):
    half = sc_ref[4]
    perm = regroup(False)
    for gr in range(8):
        y = dot(perm, x_ref[gr * 256 : (gr + 1) * 256, :]).astype(BF16)
        for r8 in range(8):
            ri, k = r8 // KB, r8 % KB
            row = ri * WINS + gr * 32
            u_ref[k, row : row + 32, :] = y[r8 * 32 : (r8 + 1) * 32]

    lane8 = lax.broadcasted_iota(jnp.int32, (8, LANES), 1)
    lane16 = lax.broadcasted_iota(jnp.int32, (16, LANES), 1)

    def one_bin(k, carry):
        later = None
        for b in range(4):
            width = 2 if b < 3 else 1
            cols = slice(b * LANES, (b + width) * LANES)
            lead = u_ref[k, :, b * LANES : (b + 1) * LANES]
            re_rows = u_ref[k, :WINS, cols]
            im_rows = u_ref[k, WINS:, cols]
            straight = jnp.concatenate([re_rows, im_rows], axis=0)
            crossed = jnp.concatenate([im_rows, -re_rows], axis=0)
            gram = dot(lead.T, jnp.concatenate([straight, crossed], axis=1))
            tiles = ([], [])
            for blk in range(8):
                a, shift = b * 8 + blk, blk * CB
                for ri in range(2):
                    base = ri * width * LANES
                    here = gram[shift : shift + 16, base : base + LANES]
                    if shift > 0:
                        if shift > HALF and width == 2:
                            there = gram[shift : shift + 16, base + LANES : base + 2 * LANES]
                            here = jnp.where(lane16 >= shift, here, there)
                        here = pltpu.roll(here, LANES - shift, 1)
                    packed = jnp.where(lane8 < HALF, here[:8], pltpu.roll(here[8:], HALF, 1))
                    packed = packed * (1.0 / WINS)
                    seen = obs_ref[a, ri, k].astype(F32)
                    live = seen < EMPTY / 2
                    slot = 1 - half if ri == 0 else half
                    corr_ref[slot, a, k] = packed.astype(BF16)
                    resid = jnp.where(live, packed - seen, 0.0)
                    spread = jnp.concatenate([resid, pltpu.roll(resid, HALF, 1)], axis=0)
                    spread = jnp.where(lane16 < HALF, spread, 0.0)
                    if shift > 0:
                        spread = pltpu.roll(spread, shift, 1)
                    if shift > HALF:
                        first = jnp.where(lane16 >= shift, spread, 0.0)
                        second = jnp.where(lane16 < shift, spread, 0.0)
                    else:
                        first, second = spread, jnp.zeros_like(spread)
                    tiles[ri].append([first, second][:width])
            res = [
                [jnp.concatenate([t[p] for t in tiles[ri]], axis=0).astype(BF16) for p in range(width)]
                for ri in range(2)
            ]
            top = jnp.concatenate([m for p in range(width) for m in (res[0][p], res[1][p])], axis=1)
            low = jnp.concatenate([m for p in range(width) for m in (-res[1][p], res[0][p])], axis=1)
            weights = jnp.concatenate([top, low], axis=0)
            waves = [
                u_ref[k, ri * WINS : (ri + 1) * WINS, (b + p) * LANES : (b + p + 1) * LANES]
                for p in range(width)
                for ri in range(2)
            ]
            pulled = dot(jnp.concatenate(waves, axis=1), weights, 1, 1)
            pushed = dot(jnp.concatenate(waves[:2], axis=1), weights)
            grad = pulled + pushed[:, :256]
            if later is not None:
                grad = grad + later
            later = pushed[:, 256:] if width == 2 else None
            d_ref[k, :WINS, b * LANES : (b + 1) * LANES] = grad[:, :LANES].astype(BF16)
            d_ref[k, WINS:, b * LANES : (b + 1) * LANES] = grad[:, LANES:].astype(BF16)
        return carry

    lax.fori_loop(0, KB, one_bin, 0)
    back = regroup(True)
    for gr in range(8):
        rows = jnp.concatenate(
            [
                d_ref[r8 % KB, (r8 // KB) * WINS + gr * 32 : (r8 // KB) * WINS + gr * 32 + 32, :]
                for r8 in range(8)
            ],
            axis=0,
        )
        out_ref[gr * 256 : (gr + 1) * 256, :] = dot(back, rows).astype(BF16)


def middle(scalars, x, obs):
    block = lambda shape: pl.BlockSpec(shape, lambda i, sc: (0,) * len(shape))
    return pl.pallas_call(
        middle_kernel,
        grid_spec=pltpu.PrefetchScalarGridSpec(
            num_scalar_prefetch=1,
            grid=(1,),
            in_specs=[block((2048, CH)), block((NB, 2, KB, 8, LANES))],
            out_specs=[block((2, NB, KB, 8, LANES)), block((2048, CH))],
            scratch_shapes=[pltpu.VMEM((KB, 2 * WINS, CH), BF16), pltpu.VMEM((KB, 2 * WINS, CH), BF16)],
        ),
        out_shape=[
            jax.ShapeDtypeStruct((2, NB, KB, 8, LANES), BF16),
            jax.ShapeDtypeStruct((2048, CH), BF16),
        ],
        compiler_params=pltpu.CompilerParams(vmem_limit_bytes=VMEM_LIMIT),
        name="middle",
    )(scalars, x, obs)


def unpack_kernel(sc_ref, x_ref, o_ref):
    perm = regroup(False, True)
    for h in range(2):
        first = sc_ref[5]
        index = first if h == 0 else 1 - first
        regrouped = []
        for gr in range(4):
            rows = x_ref[gr * 8 : (gr + 1) * 8, index].astype(F32).reshape(256, LANES).astype(BF16)
            regrouped.append(dot(perm, rows))
        for i in range(8):
            page = jnp.concatenate([r[i * 32 : (i + 1) * 32] for r in regrouped], axis=0)
            turned = page.T
            for ih in range(2):
                for s in range(SLOTS):
                    val = jnp.zeros((CB, LANES), F32)
                    for o in range(OFFSETS):
                        row = ih * HALF + o * CB
                        val = jnp.where(sc_ref[s] == o, turned[row : row + CB], val)
                    o_ref[s, ih * 8 + i, :, h * LANES : (h + 1) * LANES] = val


def unpack_correl(scalars, x):
    block = lambda shape: pl.BlockSpec(shape, lambda i, sc: (0,) * len(shape))
    return pl.pallas_call(
        unpack_kernel,
        grid_spec=pltpu.PrefetchScalarGridSpec(
            num_scalar_prefetch=1,
            grid=(1,),
            in_specs=[block((32, 2, KB, 8, LANES))],
            out_specs=block((SLOTS, CB, CB, 2 * LANES)),
        ),
        out_shape=jax.ShapeDtypeStruct((SLOTS, CB, CB, 2 * LANES), F32),
        compiler_params=pltpu.CompilerParams(vmem_limit_bytes=VMEM_LIMIT),
        name="unpack_correl",
    )(scalars, x)


def on_device(traces, pair_lists, observed):
    consts = [jnp.asarray(v) for v in table_parts()]
    g = lax.axis_index("grp")
    half, q = half_of(g), quarter_of(g)
    low = jnp.where(g < 4, 1, 0)
    scalars = jnp.concatenate([pair_lists[0], jnp.stack([2 * q + half, half, low]).astype(jnp.int32)])

    packed = pack_observed(scalars, observed[0])
    seen = lax.all_to_all(packed, "win", 0, 0)
    white, inverse = forward(traces[0], consts)
    moved = lax.all_to_all(white.reshape(WINS, 8, CH), ("win", "grp"), 0, 0)
    corr, grad = middle(scalars, moved.reshape(2048, CH), seen)
    up = lax.ppermute(corr[0], "grp", [(i, (i + 1) % GRP) for i in range(GRP)])
    down = lax.ppermute(corr[1], "grp", [(i, (i - 3) % GRP) for i in range(GRP)])
    returned = lax.all_to_all(grad.reshape(WINS, 8, CH), ("win", "grp"), 0, 0)
    up, down, returned = lax.optimization_barrier((up, down, returned))
    owned = lax.all_to_all(jnp.stack([up, down], axis=1), "win", 0, 0)
    trace_grad = backward(returned.reshape(16, 2, GRP, 8, CH), white, inverse, consts)
    correl = unpack_correl(scalars, owned)
    return correl[None], trace_grad[None]


def solution(mesh):
    return jax.shard_map(
        on_device,
        mesh=mesh,
        in_specs=(P(("win", "grp"), None, None), P("win", None), P("win", None, None, None, None)),
        out_specs=(P("win", None, None, None, "grp"), P(("win", "grp"), None, None)),
        check_vma=False,
    )
```

```python
import functools
import math

import jax
import jax.numpy as jnp
import numpy as np
from jax import lax
from jax.experimental import pallas as pl
from jax.experimental.pallas import tpu as pltpu
from jax.sharding import PartitionSpec as P

SEG = 2048
FREQ = 1024
BAND = 64
OFFSETS = 4
CB = 16
SLOTS = 3
CH = 512
WINS = 256
NB = 32
GRP = 8
KB = 4
LANES = 128
HALF = 64
EMPTY = 64.0
VMEM_LIMIT = 56 << 20

F32 = jnp.float32
BF16 = jnp.bfloat16


def half_of(g):
    return jnp.where(jnp.logical_and(g >= 3, g <= 6), 0, 1)


def quarter_of(g):
    return jnp.where(half_of(g) == 0, g - 3, (g + 1) % GRP)


def table_parts():
    row = np.arange(2 * BAND)
    j = (row % 64) // 8 * 8 + row % KB * 2 + row // 64
    imag = (row % 8) >= KB
    n = np.arange(SEG // 2)
    ang = 2.0 * math.pi * ((n[None, :] * j[:, None]) % SEG) / SEG
    a = np.where(imag[:, None], -np.sin(ang), np.cos(ang))
    b = np.where(imag[:, None], -np.cos(ang), -np.sin(ang))
    band = np.arange(FREQ // BAND)
    bang = 2.0 * math.pi * ((n[None, :] * (BAND * band[:, None])) % SEG) / SEG
    return [np.asarray(v, np.float32) for v in (a, b, np.cos(bang), np.sin(bang))]


NSC = 7


def target_slot(me, w):
    return ((me + w) % 2) * 16 + ((w // 2 - me // 2 + 4) % 4) * 4 + (w // 8 - me // 8 + 4) % 4


def source_slot(me, w):
    return ((me // 8 - w // 8 + 4) % 4) * 8 + ((me // 2 - w // 2 + 4) % 4) * 2 + (me + w) % 2


def exchange(blocks):
    def hop(array, dy, dx, dc):
        pairs = []
        for w in range(NB):
            y, x, c = w // 8, w // 2 % 4, w % 2
            pairs.append((w, ((y + dy) % 4 * 4 + (x + dx) % 4) * 2 + (c + dc) % 2))
        return lax.ppermute(array, "win", pairs)

    blocks = blocks.reshape((2, 4, 4) + blocks.shape[1:])
    blocks = jnp.stack([blocks[0], hop(blocks[1], 0, 0, 1)])
    along_x = [blocks[:, 0]] + [hop(blocks[:, d], 0, d, 0) for d in range(1, 4)]
    blocks = jnp.stack(along_x)
    along_y = [blocks[:, :, 0]] + [hop(blocks[:, :, d], d, 0, 0) for d in range(1, 4)]
    blocks = jnp.stack(along_y)
    return blocks.reshape((NB,) + blocks.shape[3:])


def dot(x, y, cx=1, cy=0):
    return lax.dot_general(x, y, (((cx,), (cy,)), ((), ())), preferred_element_type=F32)


def regroup(inverse, bins=False):
    shape = (256, 256)
    near = lax.broadcasted_iota(jnp.int32, shape, 1 if inverse else 0)
    far = lax.broadcasted_iota(jnp.int32, shape, 0 if inverse else 1)
    c = near % 32
    if bins:
        c = c // 8 * 8 + c % 2 * KB + c % 8 // 2
    return jnp.where(c * 8 + near // 32 == far, 1.0, 0.0).astype(BF16)


def full(shape):
    return pl.BlockSpec(shape, lambda *i: (0,) * len(shape))


def forward_kernel(x_ref, a_ref, b_ref, c_ref, s_ref, y_ref, r_ref, h_ref):
    step = pl.program_id(0)

    @pl.when(step == 0)
    def _():
        early = x_ref[:, : SEG // 2].astype(F32)
        late = x_ref[:, SEG // 2 :].astype(F32)
        h_ref[0] = (early + late).astype(BF16)
        h_ref[1] = (early - late).astype(BF16)

    waves = []
    for p in range(2):
        a = a_ref[p * 64 : (p + 1) * 64]
        b = b_ref[p * 64 : (p + 1) * 64]
        parts = []
        for gi in range(2):
            g = step * 2 + gi
            for wh in range(2):
                band = quarter_of(g) * 4 + half_of(g) * 2 + wh
                parts.append((a * c_ref[pl.ds(band, 1), :] + b * s_ref[pl.ds(band, 1), :]).astype(BF16))
        waves.append(dot(jnp.concatenate(parts, axis=0), h_ref[p], 1, 1))
    for gi in range(2):
        for wh in range(2):
            row = (gi * 2 + wh) * 64
            rows = [w[row : row + 64] for w in waves]
            level = jnp.sum(rows[0] * rows[0] + rows[1] * rows[1], axis=0, keepdims=True)
            inv = lax.rsqrt(level * (1.0 / BAND) + 1e-05)
            r_ref[gi, wh : wh + 1, :] = inv
            for p in range(2):
                y_ref[wh * 8 : (wh + 1) * 8, p, gi] = (rows[p] * inv).reshape(8, 8, CH).astype(BF16)


def forward(x, consts):
    return pl.pallas_call(
        forward_kernel,
        grid=(4,),
        in_specs=[full((CH, SEG)), full((128, SEG // 2)), full((128, SEG // 2)), full((16, SEG // 2)), full((16, SEG // 2))],
        out_specs=[
            pl.BlockSpec((16, 2, 2, 8, CH), lambda i: (0, 0, i, 0, 0)),
            pl.BlockSpec((2, 2, CH), lambda i: (i, 0, 0)),
        ],
        out_shape=[
            jax.ShapeDtypeStruct((16, 2, GRP, 8, CH), BF16),
            jax.ShapeDtypeStruct((GRP, 2, CH), F32),
        ],
        scratch_shapes=[pltpu.VMEM((2, CH, SEG // 2), BF16)],
        compiler_params=pltpu.CompilerParams(vmem_limit_bytes=VMEM_LIMIT),
        cost_estimate=pl.CostEstimate(flops=CH * SEG * SEG, bytes_accessed=8 << 20, transcendentals=0),
        name="forward",
    )(x, *consts)


def backward_kernel(g_ref, y_ref, r_ref, a_ref, b_ref, c_ref, s_ref, o_ref, d_ref, late_ref):
    step = pl.program_id(0)

    @pl.when(step == 0)
    def _():
        for plane in range(GRP):
            sides = ([], [])
            for wh in range(2):
                at = slice(wh * 8, (wh + 1) * 8)
                g = [g_ref[at, p, plane].astype(F32).reshape(64, CH) for p in range(2)]
                y = [y_ref[at, p, plane].astype(F32).reshape(64, CH) for p in range(2)]
                inv = r_ref[plane, wh : wh + 1, :]
                mean = jnp.sum(g[0] * y[0] + g[1] * y[1], axis=0, keepdims=True) * (1.0 / BAND)
                for p in range(2):
                    sides[p].append((g[p] - y[p] * mean) * inv)
            for p in range(2):
                turned = jnp.concatenate(sides[p], axis=0).T
                d_ref[p, :, plane * 128 : (plane + 1) * 128] = turned.astype(BF16)

    @pl.when(step % 2 == 0)
    def _():
        waves = []
        for p in range(2):
            a = a_ref[p * 64 : (p + 1) * 64]
            b = b_ref[p * 64 : (p + 1) * 64]
            parts = []
            for plane in range(GRP):
                h = 0 if 3 <= plane <= 6 else 1
                q = plane - 3 if h == 0 else (plane + 1) % GRP
                for band in (q * 4 + h * 2, q * 4 + h * 2 + 1):
                    parts.append((a * c_ref[band : band + 1, :] + b * s_ref[band : band + 1, :]).astype(BF16))
            waves.append(dot(d_ref[p], jnp.concatenate(parts, axis=0)))
        o_ref[...] = (waves[0] + waves[1]).astype(BF16)
        late_ref[...] = (waves[0] - waves[1]).astype(BF16)

    @pl.when(step % 2 == 1)
    def _():
        o_ref[...] = late_ref[...]


def backward(g, y, r, consts):
    tile = 256
    tiles = SEG // 2 // tile
    col = lambda rows: pl.BlockSpec((rows, tile), lambda i: (0, i // 2))
    return pl.pallas_call(
        backward_kernel,
        grid=(2 * tiles,),
        in_specs=[
            full((16, 2, GRP, 8, CH)),
            full((16, 2, GRP, 8, CH)),
            full((GRP, 2, CH)),
            col(128),
            col(128),
            col(16),
            col(16),
        ],
        out_specs=pl.BlockSpec((CH, tile), lambda i: (0, i // 2 + i % 2 * tiles)),
        out_shape=jax.ShapeDtypeStruct((CH, SEG), BF16),
        scratch_shapes=[pltpu.VMEM((2, CH, SEG // 2), BF16), pltpu.VMEM((CH, tile), BF16)],
        compiler_params=pltpu.CompilerParams(vmem_limit_bytes=VMEM_LIMIT),
        cost_estimate=pl.CostEstimate(flops=CH * SEG * SEG, bytes_accessed=10 << 20, transcendentals=0),
        name="backward",
    )(g, y, r, *consts)


def pack_kernel(sc_ref, re_ref, im_ref, o_ref):
    perm = regroup(True, True)
    for ri, src in enumerate((re_ref, im_ref)):
        turned = []
        for i in range(8):
            rows = []
            for ih in range(2):
                for o in range(OFFSETS):
                    val = jnp.full((CB, LANES), EMPTY, F32)
                    for s in range(SLOTS):
                        val = jnp.where(sc_ref[s] == o, src[s, ih * 8 + i], val)
                    rows.append(val)
            turned.append(jnp.concatenate(rows, axis=0).T.astype(BF16))
        for gr in range(4):
            stack = jnp.concatenate([t[gr * 32 : (gr + 1) * 32] for t in turned], axis=0)
            tile = dot(perm, stack).reshape(8, KB, 8, LANES)
            for j in range(8):
                o_ref[target_slot(sc_ref[6], gr * 8 + j), ri] = tile[j].astype(BF16)


def pack_observed(scalars, observed):
    spec = lambda base: pl.BlockSpec((SLOTS, CB, CB, LANES), lambda i, sc: (0, 0, 0, base + sc[3]))
    return pl.pallas_call(
        pack_kernel,
        grid_spec=pltpu.PrefetchScalarGridSpec(
            num_scalar_prefetch=1,
            grid=(1,),
            in_specs=[spec(0), spec(8)],
            out_specs=pl.BlockSpec((32, 2, KB, 8, LANES), lambda i, sc: (0, 0, 0, 0, 0)),
        ),
        out_shape=jax.ShapeDtypeStruct((32, 2, KB, 8, LANES), BF16),
        compiler_params=pltpu.CompilerParams(vmem_limit_bytes=VMEM_LIMIT),
        name="pack_observed",
    )(scalars, observed, observed)


def middle_kernel(sc_ref, x_ref, obs_ref, corr_ref, out_ref, u_ref, d_ref):
    half, me = sc_ref[4], sc_ref[6]
    perm = regroup(False)
    for gr in range(8):
        y = dot(perm, x_ref[gr * 256 : (gr + 1) * 256, :]).astype(BF16)
        for r8 in range(8):
            ri, k = r8 // KB, r8 % KB
            row = ri * WINS + gr * 32
            u_ref[k, row : row + 32, :] = y[r8 * 32 : (r8 + 1) * 32]

    lane8 = lax.broadcasted_iota(jnp.int32, (8, LANES), 1)
    lane16 = lax.broadcasted_iota(jnp.int32, (16, LANES), 1)

    def one_bin(k, carry):
        later = None
        for b in range(4):
            width = 2 if b < 3 else 1
            cols = slice(b * LANES, (b + width) * LANES)
            lead = u_ref[k, :, b * LANES : (b + 1) * LANES]
            re_rows = u_ref[k, :WINS, cols]
            im_rows = u_ref[k, WINS:, cols]
            straight = jnp.concatenate([re_rows, im_rows], axis=0)
            crossed = jnp.concatenate([im_rows, -re_rows], axis=0)
            gram = dot(lead.T, jnp.concatenate([straight, crossed], axis=1))
            tiles = ([], [])
            for blk in range(8):
                a, shift = b * 8 + blk, blk * CB
                for ri in range(2):
                    base = ri * width * LANES
                    here = gram[shift : shift + 16, base : base + LANES]
                    if shift > 0:
                        if shift > HALF and width == 2:
                            there = gram[shift : shift + 16, base + LANES : base + 2 * LANES]
                            here = jnp.where(lane16 >= shift, here, there)
                        here = pltpu.roll(here, LANES - shift, 1)
                    packed = jnp.where(lane8 < HALF, here[:8], pltpu.roll(here[8:], HALF, 1))
                    packed = packed * (1.0 / WINS)
                    seen = obs_ref[source_slot(me, a), ri, k].astype(F32)
                    live = seen < EMPTY / 2
                    slot = 1 - half if ri == 0 else half
                    corr_ref[target_slot(me, a), slot, k] = packed.astype(BF16)
                    resid = jnp.where(live, packed - seen, 0.0)
                    spread = jnp.concatenate([resid, pltpu.roll(resid, HALF, 1)], axis=0)
                    spread = jnp.where(lane16 < HALF, spread, 0.0)
                    if shift > 0:
                        spread = pltpu.roll(spread, shift, 1)
                    if shift > HALF:
                        first = jnp.where(lane16 >= shift, spread, 0.0)
                        second = jnp.where(lane16 < shift, spread, 0.0)
                    else:
                        first, second = spread, jnp.zeros_like(spread)
                    tiles[ri].append([first, second][:width])
            res = [
                [jnp.concatenate([t[p] for t in tiles[ri]], axis=0).astype(BF16) for p in range(width)]
                for ri in range(2)
            ]
            top = jnp.concatenate([m for p in range(width) for m in (res[0][p], res[1][p])], axis=1)
            low = jnp.concatenate([m for p in range(width) for m in (-res[1][p], res[0][p])], axis=1)
            weights = jnp.concatenate([top, low], axis=0)
            waves = [
                u_ref[k, ri * WINS : (ri + 1) * WINS, (b + p) * LANES : (b + p + 1) * LANES]
                for p in range(width)
                for ri in range(2)
            ]
            pulled = dot(jnp.concatenate(waves, axis=1), weights, 1, 1)
            pushed = dot(jnp.concatenate(waves[:2], axis=1), weights)
            grad = pulled + pushed[:, :256]
            if later is not None:
                grad = grad + later
            later = pushed[:, 256:] if width == 2 else None
            d_ref[k, :WINS, b * LANES : (b + 1) * LANES] = grad[:, :LANES].astype(BF16)
            d_ref[k, WINS:, b * LANES : (b + 1) * LANES] = grad[:, LANES:].astype(BF16)
        return carry

    lax.fori_loop(0, KB, one_bin, 0)
    back = regroup(True)
    for gr in range(8):
        rows = jnp.concatenate(
            [
                d_ref[r8 % KB, (r8 // KB) * WINS + gr * 32 : (r8 // KB) * WINS + gr * 32 + 32, :]
                for r8 in range(8)
            ],
            axis=0,
        )
        out_ref[gr * 256 : (gr + 1) * 256, :] = dot(back, rows).astype(BF16)


def middle(scalars, x, obs):
    block = lambda shape: pl.BlockSpec(shape, lambda i, sc: (0,) * len(shape))
    return pl.pallas_call(
        middle_kernel,
        grid_spec=pltpu.PrefetchScalarGridSpec(
            num_scalar_prefetch=1,
            grid=(1,),
            in_specs=[block((2048, CH)), block((NB, 2, KB, 8, LANES))],
            out_specs=[block((NB, 2, KB, 8, LANES)), block((2048, CH))],
            scratch_shapes=[pltpu.VMEM((KB, 2 * WINS, CH), BF16), pltpu.VMEM((KB, 2 * WINS, CH), BF16)],
        ),
        out_shape=[
            jax.ShapeDtypeStruct((NB, 2, KB, 8, LANES), BF16),
            jax.ShapeDtypeStruct((2048, CH), BF16),
        ],
        compiler_params=pltpu.CompilerParams(vmem_limit_bytes=VMEM_LIMIT),
        name="middle",
    )(scalars, x, obs)


def unpack_kernel(sc_ref, up_ref, down_ref, o_ref):
    perm = regroup(False, True)
    low, me = sc_ref[5], sc_ref[6]
    regrouped = ([], [])
    for gr in range(4):
        sides = []
        for ref in (up_ref, down_ref):
            rows = [ref[source_slot(me, gr * 8 + j)].astype(F32).reshape(32, LANES) for j in range(8)]
            sides.append(jnp.concatenate(rows, axis=0))
        regrouped[0].append(dot(perm, jnp.where(low == 1, sides[1], sides[0]).astype(BF16)))
        regrouped[1].append(dot(perm, jnp.where(low == 1, sides[0], sides[1]).astype(BF16)))
    for h in range(2):
        for i in range(8):
            page = jnp.concatenate([r[i * 32 : (i + 1) * 32] for r in regrouped[h]], axis=0)
            turned = page.T
            for ih in range(2):
                for s in range(SLOTS):
                    val = jnp.zeros((CB, LANES), F32)
                    for o in range(OFFSETS):
                        row = ih * HALF + o * CB
                        val = jnp.where(sc_ref[s] == o, turned[row : row + CB], val)
                    o_ref[s, ih * 8 + i, :, h * LANES : (h + 1) * LANES] = val


def unpack_correl(scalars, up, down):
    block = lambda shape: pl.BlockSpec(shape, lambda i, sc: (0,) * len(shape))
    return pl.pallas_call(
        unpack_kernel,
        grid_spec=pltpu.PrefetchScalarGridSpec(
            num_scalar_prefetch=1,
            grid=(1,),
            in_specs=[block((NB, KB, 8, LANES))] * 2,
            out_specs=block((SLOTS, CB, CB, 2 * LANES)),
        ),
        out_shape=jax.ShapeDtypeStruct((SLOTS, CB, CB, 2 * LANES), F32),
        compiler_params=pltpu.CompilerParams(vmem_limit_bytes=VMEM_LIMIT),
        name="unpack_correl",
    )(scalars, up, down)


def on_device(traces, pair_lists, observed):
    consts = [jnp.asarray(v) for v in table_parts()]
    g = lax.axis_index("grp")
    half, q = half_of(g), quarter_of(g)
    low = jnp.where(g < 4, 1, 0)
    me = lax.axis_index("win")
    scalars = jnp.concatenate([pair_lists[0], jnp.stack([2 * q + half, half, low, me]).astype(jnp.int32)])

    white, inverse = forward(traces[0], consts)
    white, scalars = lax.optimization_barrier((white, scalars))
    moved = lax.all_to_all(white.reshape(WINS, 8, CH), ("win", "grp"), 0, 0)
    seen = exchange(pack_observed(scalars, observed[0]))
    corr, grad = middle(scalars, moved.reshape(2048, CH), seen)
    returned = lax.all_to_all(grad.reshape(WINS, 8, CH), ("win", "grp"), 0, 0)
    corr = exchange(corr)
    up = lax.ppermute(corr[:, 0], "grp", [(i, (i + 1) % GRP) for i in range(GRP)])
    down = lax.ppermute(corr[:, 1], "grp", [(i, (i - 3) % GRP) for i in range(GRP)])
    trace_grad = backward(returned.reshape(16, 2, GRP, 8, CH), white, inverse, consts)
    correl = unpack_correl(scalars, up, down)
    return correl[None], trace_grad[None]


def solution(mesh):
    return jax.shard_map(
        on_device,
        mesh=mesh,
        in_specs=(P(("win", "grp"), None, None), P("win", None), P("win", None, None, None, None)),
        out_specs=(P("win", None, None, None, "grp"), P(("win", "grp"), None, None)),
        check_vma=False,
    )
```

```python
import functools
import math

import jax
import jax.numpy as jnp
import numpy as np
from jax import lax
from jax.experimental import pallas as pl
from jax.experimental.pallas import tpu as pltpu
from jax.sharding import PartitionSpec as P

SEG = 2048
FREQ = 1024
BAND = 64
OFFSETS = 4
CB = 16
SLOTS = 3
CH = 512
WINS = 256
NB = 32
GRP = 8
KB = 4
LANES = 128
HALF = 64
EMPTY = 64.0
VMEM_LIMIT = 24 << 20

F32 = jnp.float32
BF16 = jnp.bfloat16


def half_of(g):
    return jnp.where(jnp.logical_and(g >= 3, g <= 6), 0, 1)


def quarter_of(g):
    return jnp.where(half_of(g) == 0, g - 3, (g + 1) % GRP)


def table_parts():
    row = np.arange(BAND)
    j = row // 8 * 8 + row % KB * 2
    imag = (row % 8) >= KB
    n = np.arange(SEG // 2)
    ang = 2.0 * math.pi * ((n[None, :] * j[:, None]) % SEG) / SEG
    a = np.where(imag[:, None], -np.sin(ang), np.cos(ang))
    bins = np.concatenate([BAND * np.arange(FREQ // BAND), np.ones(8, np.int64)])
    turn = 2.0 * math.pi * ((n[None, :] * bins[:, None]) % SEG) / SEG
    return [np.asarray(v, np.float32) for v in (a, np.cos(turn), np.sin(turn))]


def other_part(a):
    imag = lax.broadcasted_iota(jnp.int32, a.shape, 0) % 8 >= KB
    return jnp.where(imag, -pltpu.roll(a, KB, 0), pltpu.roll(a, BAND - KB, 0))


def band_pairs(a_ref, c_ref, s_ref, cols):
    even = a_ref[:, cols]
    turned = other_part(even)
    odd = even * c_ref[16:17, cols] + turned * s_ref[16:17, cols]
    return (even, turned), (odd, other_part(odd))


NSC = 7


def target_slot(me, w):
    return ((me + w) % 2) * 16 + ((w // 2 - me // 2 + 4) % 4) * 4 + (w // 8 - me // 8 + 4) % 4


def source_slot(me, w):
    return ((me // 8 - w // 8 + 4) % 4) * 8 + ((me // 2 - w // 2 + 4) % 4) * 2 + (me + w) % 2


def exchange(blocks):
    def hop(array, dy, dx, dc):
        pairs = []
        for w in range(NB):
            y, x, c = w // 8, w // 2 % 4, w % 2
            pairs.append((w, ((y + dy) % 4 * 4 + (x + dx) % 4) * 2 + (c + dc) % 2))
        return lax.ppermute(array, "win", pairs)

    blocks = blocks.reshape((2, 4, 4) + blocks.shape[1:])
    blocks = jnp.stack([blocks[0], hop(blocks[1], 0, 0, 1)])
    along_x = [blocks[:, 0]] + [hop(blocks[:, d], 0, d, 0) for d in range(1, 4)]
    blocks = jnp.stack(along_x)
    along_y = [blocks[:, :, 0]] + [hop(blocks[:, :, d], d, 0, 0) for d in range(1, 4)]
    blocks = jnp.stack(along_y)
    return blocks.reshape((NB,) + blocks.shape[3:])


def dot(x, y, cx=1, cy=0):
    return lax.dot_general(x, y, (((cx,), (cy,)), ((), ())), preferred_element_type=F32)


def regroup(inverse, bins=False):
    shape = (256, 256)
    near = lax.broadcasted_iota(jnp.int32, shape, 1 if inverse else 0)
    far = lax.broadcasted_iota(jnp.int32, shape, 0 if inverse else 1)
    c = near % 32
    if bins:
        c = c // 8 * 8 + c % 2 * KB + c % 8 // 2
    return jnp.where(c * 8 + near // 32 == far, 1.0, 0.0).astype(BF16)


def full(shape):
    return pl.BlockSpec(shape, lambda *i: (0,) * len(shape))


def plane_bands(g):
    h = 0 if 3 <= g <= 6 else 1
    q = g - 3 if h == 0 else (g + 1) % GRP
    return (q * 4 + h * 2, q * 4 + h * 2 + 1)


def forward_kernel(x_ref, a_ref, c_ref, s_ref, y_hbm, r_ref, y_ref, sem):
    copies = []
    early = x_ref[:, : SEG // 2].astype(F32)
    late = x_ref[:, SEG // 2 :].astype(F32)
    pairs = band_pairs(a_ref, c_ref, s_ref, slice(None))
    halves = ((early + late).astype(BF16), (early - late).astype(BF16))
    for step in range(4):
        waves = []
        for p in range(2):
            a, b = pairs[p]
            parts = []
            for g in (step * 2, step * 2 + 1):
                for band in plane_bands(g):
                    parts.append((a * c_ref[band : band + 1, :] + b * s_ref[band : band + 1, :]).astype(BF16))
            waves.append(dot(jnp.concatenate(parts, axis=0), halves[p], 1, 1))
        for gi in range(2):
            for wh in range(2):
                row = (gi * 2 + wh) * 64
                rows = [w[row : row + 64] for w in waves]
                level = jnp.sum(rows[0] * rows[0] + rows[1] * rows[1], axis=0, keepdims=True)
                inv = lax.rsqrt(level * (1.0 / BAND) + 1e-05)
                r_ref[step * 2 + gi, wh : wh + 1, :] = inv
                for p in range(2):
                    tile = (rows[p] * inv).reshape(8, 8, CH).astype(BF16)
                    y_ref[wh * 8 : (wh + 1) * 8, p, step * 2 + gi] = tile
        planes = (slice(None), slice(None), slice(step * 2, step * 2 + 2))
        copy = pltpu.make_async_copy(y_ref.at[planes], y_hbm.at[planes], sem.at[step])
        copy.start()
        copies.append(copy)
    for copy in copies:
        copy.wait()


IN_VMEM = pl.BlockSpec(memory_space=pltpu.VMEM)
IN_HBM = pl.BlockSpec(memory_space=pltpu.HBM)
IN_SMEM = pl.BlockSpec(memory_space=pltpu.SMEM)


def forward(x, consts):
    return pl.pallas_call(
        forward_kernel,
        in_specs=[IN_VMEM] * 4,
        out_specs=[IN_HBM, IN_VMEM],
        out_shape=[
            pltpu.HBM((16, 2, GRP, 8, CH), BF16),
            jax.ShapeDtypeStruct((GRP, 2, CH), F32),
        ],
        scratch_shapes=[pltpu.VMEM((16, 2, GRP, 8, CH), BF16), pltpu.SemaphoreType.DMA((4,))],
        compiler_params=pltpu.CompilerParams(vmem_limit_bytes=VMEM_LIMIT),
        cost_estimate=pl.CostEstimate(flops=CH * SEG * SEG, bytes_accessed=8 << 20, transcendentals=0),
        name="forward",
    )(x, *consts)


def backward_kernel(g_hbm, y_ref, r_ref, a_ref, c_ref, s_ref, o_ref, g_ref, d_ref, stage_ref, sem):
    loads = []
    for step in range(4):
        planes = (slice(None), slice(None), slice(step * 2, step * 2 + 2))
        load = pltpu.make_async_copy(g_hbm.at[planes], g_ref.at[planes], sem.at[8 + step])
        load.start()
        loads.append(load)
    for plane in range(GRP):
        if plane % 2 == 0:
            loads[plane // 2].wait()
        sides = ([], [])
        for wh in range(2):
            at = slice(wh * 8, (wh + 1) * 8)
            g = [g_ref[at, p, plane].astype(F32).reshape(64, CH) for p in range(2)]
            y = [y_ref[at, p, plane].astype(F32).reshape(64, CH) for p in range(2)]
            inv = r_ref[plane, wh : wh + 1, :]
            mean = jnp.sum(g[0] * y[0] + g[1] * y[1], axis=0, keepdims=True) * (1.0 / BAND)
            for p in range(2):
                sides[p].append((g[p] - y[p] * mean) * inv)
        for p in range(2):
            turned = jnp.concatenate(sides[p], axis=0).astype(BF16).T
            d_ref[p, :, plane * 128 : (plane + 1) * 128] = turned

    tile = 256
    tiles = SEG // 2 // tile
    copies = []
    for t in range(tiles):
        cols = slice(t * tile, (t + 1) * tile)
        pairs = band_pairs(a_ref, c_ref, s_ref, cols)
        waves = []
        for p in range(2):
            a, b = pairs[p]
            parts = []
            for plane in range(GRP):
                for band in plane_bands(plane):
                    c = c_ref[band : band + 1, cols]
                    s = s_ref[band : band + 1, cols]
                    parts.append((a * c + b * s).astype(BF16))
            waves.append(dot(d_ref[p], jnp.concatenate(parts, axis=0)))
        stage_ref[2 * t] = (waves[0] + waves[1]).astype(BF16)
        stage_ref[2 * t + 1] = (waves[0] - waves[1]).astype(BF16)
        for part in range(2):
            to = o_ref.at[:, pl.ds(part * (SEG // 2) + t * tile, tile)]
            copy = pltpu.make_async_copy(stage_ref.at[2 * t + part], to, sem.at[2 * t + part])
            copy.start()
            copies.append(copy)
    for copy in copies:
        copy.wait()


def backward(g, y, r, consts):
    return pl.pallas_call(
        backward_kernel,
        in_specs=[IN_HBM] + [IN_VMEM] * 5,
        out_specs=pl.BlockSpec(memory_space=pl.ANY),
        out_shape=jax.ShapeDtypeStruct((CH, SEG), BF16),
        scratch_shapes=[
            pltpu.VMEM((16, 2, GRP, 8, CH), BF16),
            pltpu.VMEM((2, CH, SEG // 2), BF16),
            pltpu.VMEM((8, CH, 256), BF16),
            pltpu.SemaphoreType.DMA((12,)),
        ],
        compiler_params=pltpu.CompilerParams(vmem_limit_bytes=VMEM_LIMIT),
        cost_estimate=pl.CostEstimate(flops=CH * SEG * SEG, bytes_accessed=10 << 20, transcendentals=0),
        name="backward",
    )(g, y, r, *consts)


def pack_kernel(sc_ref, re_ref, im_ref, o_ref):
    perm = regroup(True, True)
    for ri, src in enumerate((re_ref, im_ref)):
        turned = []
        for i in range(8):
            rows = []
            for ih in range(2):
                for o in range(OFFSETS):
                    val = jnp.full((CB, LANES), EMPTY, F32)
                    for s in range(SLOTS):
                        val = jnp.where(sc_ref[s] == o, src[s, ih * 8 + i], val)
                    rows.append(val)
            turned.append(jnp.concatenate(rows, axis=0).T.astype(BF16))
        for gr in range(4):
            stack = jnp.concatenate([t[gr * 32 : (gr + 1) * 32] for t in turned], axis=0)
            tile = dot(perm, stack).reshape(8, KB, 8, LANES)
            for j in range(8):
                o_ref[target_slot(sc_ref[6], gr * 8 + j), ri] = tile[j].astype(BF16)


def pack_observed(scalars, observed):
    spec = lambda base: pl.BlockSpec((SLOTS, CB, CB, LANES), lambda i, sc: (0, 0, 0, base + sc[3]))
    return pl.pallas_call(
        pack_kernel,
        grid_spec=pltpu.PrefetchScalarGridSpec(
            num_scalar_prefetch=1,
            grid=(1,),
            in_specs=[spec(0), spec(8)],
            out_specs=pl.BlockSpec((32, 2, KB, 8, LANES), lambda i, sc: (0, 0, 0, 0, 0)),
        ),
        out_shape=jax.ShapeDtypeStruct((32, 2, KB, 8, LANES), BF16),
        compiler_params=pltpu.CompilerParams(vmem_limit_bytes=VMEM_LIMIT),
        name="pack_observed",
    )(scalars, observed, observed)


def middle_kernel(sc_ref, x_ref, obs_ref, corr_ref, out_hbm, u_ref, d_ref, out_ref, sem):
    half, me = sc_ref[4], sc_ref[6]
    perm = regroup(False)
    for gr in range(8):
        y = dot(perm, x_ref[gr * 256 : (gr + 1) * 256, :]).astype(BF16)
        for r8 in range(8):
            ri, k = r8 // KB, r8 % KB
            row = ri * WINS + gr * 32
            u_ref[k, row : row + 32, :] = y[r8 * 32 : (r8 + 1) * 32]

    lane8 = lax.broadcasted_iota(jnp.int32, (8, LANES), 1)
    lane16 = lax.broadcasted_iota(jnp.int32, (16, LANES), 1)

    def one_bin(k):
        later = None
        for b in range(4):
            width = 2 if b < 3 else 1
            cols = slice(b * LANES, (b + width) * LANES)
            lead = u_ref[k, :, b * LANES : (b + 1) * LANES]
            re_rows = u_ref[k, :WINS, cols]
            im_rows = u_ref[k, WINS:, cols]
            straight = jnp.concatenate([re_rows, im_rows], axis=0)
            crossed = jnp.concatenate([im_rows, -re_rows], axis=0)
            gram = dot(lead.T, jnp.concatenate([straight, crossed], axis=1))
            tiles = ([], [])
            for blk in range(8):
                a, shift = b * 8 + blk, blk * CB
                for ri in range(2):
                    base = ri * width * LANES
                    here = gram[shift : shift + 16, base : base + LANES]
                    if shift > 0:
                        if shift > HALF and width == 2:
                            there = gram[shift : shift + 16, base + LANES : base + 2 * LANES]
                            here = jnp.where(lane16 >= shift, here, there)
                        here = pltpu.roll(here, LANES - shift, 1)
                    packed = jnp.where(lane8 < HALF, here[:8], pltpu.roll(here[8:], HALF, 1))
                    packed = packed * (1.0 / WINS)
                    seen = obs_ref[source_slot(me, a), ri, k].astype(F32)
                    live = seen < EMPTY / 2
                    slot = 1 - half if ri == 0 else half
                    corr_ref[target_slot(me, a), slot, k] = packed.astype(BF16)
                    resid = jnp.where(live, packed - seen, 0.0)
                    spread = jnp.concatenate([resid, pltpu.roll(resid, HALF, 1)], axis=0)
                    spread = jnp.where(lane16 < HALF, spread, 0.0)
                    if shift > 0:
                        spread = pltpu.roll(spread, shift, 1)
                    if shift > HALF:
                        first = jnp.where(lane16 >= shift, spread, 0.0)
                        second = jnp.where(lane16 < shift, spread, 0.0)
                    else:
                        first, second = spread, jnp.zeros_like(spread)
                    tiles[ri].append([first, second][:width])
            res = [
                [jnp.concatenate([t[p] for t in tiles[ri]], axis=0).astype(BF16) for p in range(width)]
                for ri in range(2)
            ]
            top = jnp.concatenate([m for p in range(width) for m in (res[0][p], res[1][p])], axis=1)
            low = jnp.concatenate([m for p in range(width) for m in (-res[1][p], res[0][p])], axis=1)
            weights = jnp.concatenate([top, low], axis=0)
            waves = [
                u_ref[k, ri * WINS : (ri + 1) * WINS, (b + p) * LANES : (b + p + 1) * LANES]
                for p in range(width)
                for ri in range(2)
            ]
            pulled = dot(jnp.concatenate(waves, axis=1), weights, 1, 1)
            pushed = dot(jnp.concatenate(waves[:2], axis=1), weights)
            grad = pulled + pushed[:, :256]
            if later is not None:
                grad = grad + later
            later = pushed[:, 256:] if width == 2 else None
            d_ref[k, :WINS, b * LANES : (b + 1) * LANES] = grad[:, :LANES].astype(BF16)
            d_ref[k, WINS:, b * LANES : (b + 1) * LANES] = grad[:, LANES:].astype(BF16)

    for k in range(KB):
        one_bin(k)
    back = regroup(True)
    copies = []
    for gr in range(8):
        rows = jnp.concatenate(
            [
                d_ref[r8 % KB, (r8 // KB) * WINS + gr * 32 : (r8 // KB) * WINS + gr * 32 + 32, :]
                for r8 in range(8)
            ],
            axis=0,
        )
        place = slice(gr * 256, (gr + 1) * 256)
        out_ref[place, :] = dot(back, rows).astype(BF16)
        copy = pltpu.make_async_copy(out_ref.at[place, :], out_hbm.at[place, :], sem.at[gr])
        copy.start()
        copies.append(copy)
    for copy in copies:
        copy.wait()


def middle(scalars, x, obs):
    return pl.pallas_call(
        middle_kernel,
        in_specs=[IN_SMEM, IN_VMEM, IN_VMEM],
        out_specs=[IN_VMEM, IN_HBM],
        scratch_shapes=[
            pltpu.VMEM((KB, 2 * WINS, CH), BF16),
            pltpu.VMEM((KB, 2 * WINS, CH), BF16),
            pltpu.VMEM((2048, CH), BF16),
            pltpu.SemaphoreType.DMA((8,)),
        ],
        out_shape=[
            jax.ShapeDtypeStruct((NB, 2, KB, 8, LANES), BF16),
            pltpu.HBM((2048, CH), BF16),
        ],
        compiler_params=pltpu.CompilerParams(vmem_limit_bytes=VMEM_LIMIT),
        name="middle",
    )(scalars, x, obs)


def unpack_kernel(sc_ref, up_ref, down_ref, o_ref):
    perm = regroup(False, True)
    low, me = sc_ref[5], sc_ref[6]
    regrouped = ([], [])
    for gr in range(4):
        sides = []
        for ref in (up_ref, down_ref):
            rows = [ref[source_slot(me, gr * 8 + j)].astype(F32).reshape(32, LANES) for j in range(8)]
            sides.append(jnp.concatenate(rows, axis=0))
        regrouped[0].append(dot(perm, jnp.where(low == 1, sides[1], sides[0]).astype(BF16)))
        regrouped[1].append(dot(perm, jnp.where(low == 1, sides[0], sides[1]).astype(BF16)))
    for h in range(2):
        for i in range(8):
            page = jnp.concatenate([r[i * 32 : (i + 1) * 32] for r in regrouped[h]], axis=0)
            turned = page.T
            for ih in range(2):
                for s in range(SLOTS):
                    val = jnp.zeros((CB, LANES), F32)
                    for o in range(OFFSETS):
                        row = ih * HALF + o * CB
                        val = jnp.where(sc_ref[s] == o, turned[row : row + CB], val)
                    o_ref[s, ih * 8 + i, :, h * LANES : (h + 1) * LANES] = val


def unpack_correl(scalars, up, down):
    block = lambda shape: pl.BlockSpec(shape, lambda i, sc: (0,) * len(shape))
    return pl.pallas_call(
        unpack_kernel,
        grid_spec=pltpu.PrefetchScalarGridSpec(
            num_scalar_prefetch=1,
            grid=(1,),
            in_specs=[block((NB, KB, 8, LANES))] * 2,
            out_specs=block((SLOTS, CB, CB, 2 * LANES)),
        ),
        out_shape=jax.ShapeDtypeStruct((SLOTS, CB, CB, 2 * LANES), F32),
        compiler_params=pltpu.CompilerParams(vmem_limit_bytes=VMEM_LIMIT),
        name="unpack_correl",
    )(scalars, up, down)


def on_device(traces, pair_lists, observed):
    consts = [jnp.asarray(v) for v in table_parts()]
    white, inverse = forward(traces[0], consts)
    white, pair_lists = lax.optimization_barrier((white, pair_lists))
    g, me = lax.axis_index("grp"), lax.axis_index("win")
    half, q = half_of(g), quarter_of(g)
    low = jnp.where(g < 4, 1, 0)
    scalars = jnp.concatenate([pair_lists[0], jnp.stack([2 * q + half, half, low, me]).astype(jnp.int32)])
    moved = lax.all_to_all(white.reshape(WINS, 8, CH), ("win", "grp"), 0, 0)
    seen = exchange(pack_observed(scalars, observed[0]))
    corr, grad = middle(scalars, moved.reshape(2048, CH), seen)
    returned = lax.all_to_all(grad.reshape(WINS, 8, CH), ("win", "grp"), 0, 0)
    corr = exchange(corr)
    up = lax.ppermute(corr[:, 0], "grp", [(i, (i + 1) % GRP) for i in range(GRP)])
    down = lax.ppermute(corr[:, 1], "grp", [(i, (i - 3) % GRP) for i in range(GRP)])
    trace_grad = backward(returned.reshape(16, 2, GRP, 8, CH), white, inverse, consts)
    up, down, trace_grad = lax.optimization_barrier((up, down, trace_grad))
    correl = unpack_correl(scalars, up, down)
    return correl[None], trace_grad[None]


def solution(mesh):
    return jax.shard_map(
        on_device,
        mesh=mesh,
        in_specs=(P(("win", "grp"), None, None), P("win", None), P("win", None, None, None, None)),
        out_specs=(P("win", None, None, None, "grp"), P(("win", "grp"), None, None)),
        check_vma=False,
    )
```

```python
import functools
import math

import jax
import jax.numpy as jnp
import numpy as np
from jax import lax
from jax.experimental import pallas as pl
from jax.experimental.pallas import tpu as pltpu
from jax.sharding import PartitionSpec as P

SEG = 2048
FREQ = 1024
BAND = 64
OFFSETS = 4
CB = 16
SLOTS = 3
CH = 512
WINS = 256
NB = 32
GRP = 8
KB = 4
LANES = 128
HALF = 64
EMPTY = 64.0
VMEM_LIMIT = 24 << 20

F32 = jnp.float32
BF16 = jnp.bfloat16


def half_of(g):
    return jnp.where(jnp.logical_and(g >= 3, g <= 6), 0, 1)


def quarter_of(g):
    return jnp.where(half_of(g) == 0, g - 3, (g + 1) % GRP)


def table_parts():
    row = np.arange(BAND)
    j = row // 8 * 8 + row % KB * 2
    imag = (row % 8) >= KB
    n = np.arange(SEG // 2)
    ang = 2.0 * math.pi * ((n[None, :] * j[:, None]) % SEG) / SEG
    a = np.where(imag[:, None], -np.sin(ang), np.cos(ang))
    bins = np.concatenate([BAND * np.arange(FREQ // BAND), np.ones(8, np.int64)])
    turn = 2.0 * math.pi * ((n[None, :] * bins[:, None]) % SEG) / SEG
    return [np.asarray(v, np.float32) for v in (a, np.cos(turn), np.sin(turn))]


def other_part(a):
    imag = lax.broadcasted_iota(jnp.int32, a.shape, 0) % 8 >= KB
    return jnp.where(imag, -pltpu.roll(a, KB, 0), pltpu.roll(a, BAND - KB, 0))


def band_pairs(a_ref, c_ref, s_ref, cols):
    even = a_ref[:, cols]
    turned = other_part(even)
    odd = even * c_ref[16:17, cols] + turned * s_ref[16:17, cols]
    return (even, turned), (odd, other_part(odd))


NSC = 7


def target_slot(me, w):
    return ((me + w) % 2) * 16 + ((w // 2 - me // 2 + 4) % 4) * 4 + (w // 8 - me // 8 + 4) % 4


def source_slot(me, w):
    return ((me // 8 - w // 8 + 4) % 4) * 8 + ((me // 2 - w // 2 + 4) % 4) * 2 + (me + w) % 2


def exchange(blocks):
    def hop(array, dy, dx, dc):
        pairs = []
        for w in range(NB):
            y, x, c = w // 8, w // 2 % 4, w % 2
            pairs.append((w, ((y + dy) % 4 * 4 + (x + dx) % 4) * 2 + (c + dc) % 2))
        return lax.ppermute(array, "win", pairs)

    blocks = blocks.reshape((2, 4, 4) + blocks.shape[1:])
    blocks = jnp.stack([blocks[0], hop(blocks[1], 0, 0, 1)])
    along_x = [blocks[:, 0]] + [hop(blocks[:, d], 0, d, 0) for d in range(1, 4)]
    blocks = jnp.stack(along_x)
    along_y = [blocks[:, :, 0]] + [hop(blocks[:, :, d], d, 0, 0) for d in range(1, 4)]
    blocks = jnp.stack(along_y)
    return blocks.reshape((NB,) + blocks.shape[3:])


def dot(x, y, cx=1, cy=0):
    return lax.dot_general(x, y, (((cx,), (cy,)), ((), ())), preferred_element_type=F32)


def regroup(inverse, bins=False):
    shape = (256, 256)
    near = lax.broadcasted_iota(jnp.int32, shape, 1 if inverse else 0)
    far = lax.broadcasted_iota(jnp.int32, shape, 0 if inverse else 1)
    c = near % 32
    if bins:
        c = c // 8 * 8 + c % 2 * KB + c % 8 // 2
    return jnp.where(c * 8 + near // 32 == far, 1.0, 0.0).astype(BF16)


def full(shape):
    return pl.BlockSpec(shape, lambda *i: (0,) * len(shape))


def plane_bands(g):
    h = 0 if 3 <= g <= 6 else 1
    q = g - 3 if h == 0 else (g + 1) % GRP
    return (q * 4 + h * 2, q * 4 + h * 2 + 1)


def forward_kernel(x_hbm, a_hbm, c_hbm, s_hbm, y_hbm, r_ref, x_ref, a_ref, c_ref, s_ref, y_ref, sem):
    pieces = [(a_hbm, a_ref), (c_hbm, c_ref), (s_hbm, s_ref)]
    for i in range(4):
        rows = slice(i * 128, (i + 1) * 128)
        pieces.append((x_hbm.at[rows, :], x_ref.at[rows, :]))
    loads = [pltpu.make_async_copy(src, dst, sem.at[4 + i]) for i, (src, dst) in enumerate(pieces)]
    for load in loads:
        load.start()
    for load in loads[:3]:
        load.wait()
    pairs = band_pairs(a_ref, c_ref, s_ref, slice(None))

    def tables(step):
        for a, b in pairs:
            parts = []
            for g in (step * 2, step * 2 + 1):
                for band in plane_bands(g):
                    parts.append((a * c_ref[band : band + 1, :] + b * s_ref[band : band + 1, :]).astype(BF16))
            yield jnp.concatenate(parts, axis=0)

    ahead = list(tables(0))
    for load in loads[3:]:
        load.wait()
    early = x_ref[:, : SEG // 2].astype(F32)
    late = x_ref[:, SEG // 2 :].astype(F32)
    halves = ((early + late).astype(BF16), (early - late).astype(BF16))
    copies = []
    for step in range(4):
        waves = [dot(ahead[p], halves[p], 1, 1) for p in range(2)]
        if step < 3:
            ahead = list(tables(step + 1))
        for gi in range(2):
            for wh in range(2):
                row = (gi * 2 + wh) * 64
                rows = [w[row : row + 64] for w in waves]
                level = jnp.sum(rows[0] * rows[0] + rows[1] * rows[1], axis=0, keepdims=True)
                inv = lax.rsqrt(level * (1.0 / BAND) + 1e-05)
                r_ref[step * 2 + gi, wh : wh + 1, :] = inv
                for p in range(2):
                    tile = (rows[p] * inv).reshape(8, 8, CH).astype(BF16)
                    y_ref[wh * 8 : (wh + 1) * 8, p, step * 2 + gi] = tile
        planes = (slice(None), slice(None), slice(step * 2, step * 2 + 2))
        copy = pltpu.make_async_copy(y_ref.at[planes], y_hbm.at[planes], sem.at[step])
        copy.start()
        copies.append(copy)
    for copy in copies:
        copy.wait()


IN_HBM = pl.BlockSpec(memory_space=pltpu.HBM)
IN_VMEM = pl.BlockSpec(memory_space=pltpu.VMEM)
IN_SMEM = pl.BlockSpec(memory_space=pltpu.SMEM)


def forward(x, consts):
    return pl.pallas_call(
        forward_kernel,
        in_specs=[IN_HBM] * 4,
        out_specs=[IN_HBM, IN_VMEM],
        out_shape=[
            pltpu.HBM((16, 2, GRP, 8, CH), BF16),
            jax.ShapeDtypeStruct((GRP, 2, CH), F32),
        ],
        scratch_shapes=[
            pltpu.VMEM((CH, SEG), BF16),
            pltpu.VMEM((BAND, SEG // 2), F32),
            pltpu.VMEM((24, SEG // 2), F32),
            pltpu.VMEM((24, SEG // 2), F32),
            pltpu.VMEM((16, 2, GRP, 8, CH), BF16),
            pltpu.SemaphoreType.DMA((11,)),
        ],
        compiler_params=pltpu.CompilerParams(vmem_limit_bytes=VMEM_LIMIT),
        cost_estimate=pl.CostEstimate(flops=CH * SEG * SEG, bytes_accessed=8 << 20, transcendentals=0),
        name="forward",
    )(*(pltpu.with_memory_space_constraint(v, pltpu.HBM) for v in (x, *consts)))


def backward_kernel(g_hbm, y_ref, r_ref, a_ref, c_ref, s_ref, o_ref, g_ref, d_ref, stage_ref, sem):
    loads = []
    for step in range(4):
        planes = (slice(None), slice(None), slice(step * 2, step * 2 + 2))
        load = pltpu.make_async_copy(g_hbm.at[planes], g_ref.at[planes], sem.at[8 + step])
        load.start()
        loads.append(load)
    for plane in range(GRP):
        if plane % 2 == 0:
            loads[plane // 2].wait()
        sides = ([], [])
        for wh in range(2):
            at = slice(wh * 8, (wh + 1) * 8)
            g = [g_ref[at, p, plane].astype(F32).reshape(64, CH) for p in range(2)]
            y = [y_ref[at, p, plane].astype(F32).reshape(64, CH) for p in range(2)]
            inv = r_ref[plane, wh : wh + 1, :]
            mean = jnp.sum(g[0] * y[0] + g[1] * y[1], axis=0, keepdims=True) * (1.0 / BAND)
            for p in range(2):
                sides[p].append((g[p] - y[p] * mean) * inv)
        for p in range(2):
            turned = jnp.concatenate(sides[p], axis=0).astype(BF16).T
            d_ref[p, :, plane * 128 : (plane + 1) * 128] = turned

    tile = 256
    tiles = SEG // 2 // tile
    copies = []
    for t in range(tiles):
        cols = slice(t * tile, (t + 1) * tile)
        pairs = band_pairs(a_ref, c_ref, s_ref, cols)
        waves = []
        for p in range(2):
            a, b = pairs[p]
            parts = []
            for plane in range(GRP):
                for band in plane_bands(plane):
                    c = c_ref[band : band + 1, cols]
                    s = s_ref[band : band + 1, cols]
                    parts.append((a * c + b * s).astype(BF16))
            waves.append(dot(d_ref[p], jnp.concatenate(parts, axis=0)))
        stage_ref[2 * t] = (waves[0] + waves[1]).astype(BF16)
        stage_ref[2 * t + 1] = (waves[0] - waves[1]).astype(BF16)
        for part in range(2):
            to = o_ref.at[:, pl.ds(part * (SEG // 2) + t * tile, tile)]
            copy = pltpu.make_async_copy(stage_ref.at[2 * t + part], to, sem.at[2 * t + part])
            copy.start()
            copies.append(copy)
    for copy in copies:
        copy.wait()


def backward(g, y, r, consts):
    return pl.pallas_call(
        backward_kernel,
        in_specs=[IN_HBM] + [IN_VMEM] * 5,
        out_specs=pl.BlockSpec(memory_space=pl.ANY),
        out_shape=jax.ShapeDtypeStruct((CH, SEG), BF16),
        scratch_shapes=[
            pltpu.VMEM((16, 2, GRP, 8, CH), BF16),
            pltpu.VMEM((2, CH, SEG // 2), BF16),
            pltpu.VMEM((8, CH, 256), BF16),
            pltpu.SemaphoreType.DMA((12,)),
        ],
        compiler_params=pltpu.CompilerParams(vmem_limit_bytes=VMEM_LIMIT),
        cost_estimate=pl.CostEstimate(flops=CH * SEG * SEG, bytes_accessed=10 << 20, transcendentals=0),
        name="backward",
    )(g, y, r, *consts)


def pack_kernel(sc_ref, re_ref, im_ref, o_ref):
    perm = regroup(True, True)
    for ri, src in enumerate((re_ref, im_ref)):
        turned = []
        for i in range(8):
            rows = []
            for ih in range(2):
                for o in range(OFFSETS):
                    val = jnp.full((CB, LANES), EMPTY, F32)
                    for s in range(SLOTS):
                        val = jnp.where(sc_ref[s] == o, src[s, ih * 8 + i], val)
                    rows.append(val)
            turned.append(jnp.concatenate(rows, axis=0).T.astype(BF16))
        for gr in range(4):
            stack = jnp.concatenate([t[gr * 32 : (gr + 1) * 32] for t in turned], axis=0)
            tile = dot(perm, stack).reshape(8, KB, 8, LANES)
            for j in range(8):
                o_ref[target_slot(sc_ref[6], gr * 8 + j), ri] = tile[j].astype(BF16)


def pack_observed(scalars, observed):
    spec = lambda base: pl.BlockSpec((SLOTS, CB, CB, LANES), lambda i, sc: (0, 0, 0, base + sc[3]))
    return pl.pallas_call(
        pack_kernel,
        grid_spec=pltpu.PrefetchScalarGridSpec(
            num_scalar_prefetch=1,
            grid=(1,),
            in_specs=[spec(0), spec(8)],
            out_specs=pl.BlockSpec((32, 2, KB, 8, LANES), lambda i, sc: (0, 0, 0, 0, 0)),
        ),
        out_shape=jax.ShapeDtypeStruct((32, 2, KB, 8, LANES), BF16),
        compiler_params=pltpu.CompilerParams(vmem_limit_bytes=VMEM_LIMIT),
        name="pack_observed",
    )(scalars, observed, observed)


def middle_kernel(sc_ref, x_ref, obs_ref, corr_ref, out_hbm, u_ref, d_ref, out_ref, sem):
    half, me = sc_ref[4], sc_ref[6]
    perm = regroup(False)
    for gr in range(8):
        y = dot(perm, x_ref[gr * 256 : (gr + 1) * 256, :]).astype(BF16)
        for r8 in range(8):
            ri, k = r8 // KB, r8 % KB
            row = ri * WINS + gr * 32
            u_ref[k, row : row + 32, :] = y[r8 * 32 : (r8 + 1) * 32]

    lane8 = lax.broadcasted_iota(jnp.int32, (8, LANES), 1)
    lane16 = lax.broadcasted_iota(jnp.int32, (16, LANES), 1)

    def correlate(k, b, width):
        cols = slice(b * LANES, (b + width) * LANES)
        lead = u_ref[k, :, b * LANES : (b + 1) * LANES]
        re_rows = u_ref[k, :WINS, cols]
        im_rows = u_ref[k, WINS:, cols]
        straight = jnp.concatenate([re_rows, im_rows], axis=0)
        crossed = jnp.concatenate([im_rows, -re_rows], axis=0)
        return dot(lead.T, jnp.concatenate([straight, crossed], axis=1))

    def weigh(k, b, width, gram):
        tiles = ([], [])
        for blk in range(8):
            a, shift = b * 8 + blk, blk * CB
            source, target = source_slot(me, a), target_slot(me, a)
            for ri in range(2):
                base = ri * width * LANES
                here = gram[shift : shift + 16, base : base + LANES]
                if shift > 0:
                    if shift > HALF and width == 2:
                        there = gram[shift : shift + 16, base + LANES : base + 2 * LANES]
                        here = jnp.where(lane16 >= shift, here, there)
                    here = pltpu.roll(here, LANES - shift, 1)
                packed = jnp.where(lane8 < HALF, here[:8], pltpu.roll(here[8:], HALF, 1))
                packed = packed * (1.0 / WINS)
                seen = obs_ref[source, ri, k].astype(F32)
                corr_ref[target, 1 - half if ri == 0 else half, k] = packed.astype(BF16)
                resid = jnp.where(seen < EMPTY / 2, packed - seen, 0.0)
                spread = jnp.concatenate([resid, pltpu.roll(resid, HALF, 1)], axis=0)
                spread = jnp.where(lane16 < HALF, spread, 0.0)
                if shift > 0:
                    spread = pltpu.roll(spread, shift, 1)
                if shift > HALF:
                    first = jnp.where(lane16 >= shift, spread, 0.0)
                    second = jnp.where(lane16 < shift, spread, 0.0)
                else:
                    first, second = spread, jnp.zeros_like(spread)
                tiles[ri].append([first, second][:width])
        res = [
            [jnp.concatenate([t[p] for t in tiles[ri]], axis=0).astype(BF16) for p in range(width)]
            for ri in range(2)
        ]
        top = jnp.concatenate([m for p in range(width) for m in (res[0][p], res[1][p])], axis=1)
        low = jnp.concatenate([m for p in range(width) for m in (-res[1][p], res[0][p])], axis=1)
        return jnp.concatenate([top, low], axis=0)

    def pull(k, b, width, weights, later):
        waves = [
            u_ref[k, ri * WINS : (ri + 1) * WINS, (b + p) * LANES : (b + p + 1) * LANES]
            for p in range(width)
            for ri in range(2)
        ]
        pushed = dot(jnp.concatenate(waves[:2], axis=1), weights)
        grad = dot(jnp.concatenate(waves, axis=1), weights, 1, 1) + pushed[:, :256]
        if b > 0:
            grad = grad + later
        d_ref[k, :WINS, b * LANES : (b + 1) * LANES] = grad[:, :LANES].astype(BF16)
        d_ref[k, WINS:, b * LANES : (b + 1) * LANES] = grad[:, LANES:].astype(BF16)
        return pushed[:, 256:]

    steps = [(k, b, 2 if b < 3 else 1) for k in range(KB) for b in range(4)]
    gram, weights, later = correlate(*steps[0]), None, None
    for i in range(len(steps) + 1):
        ahead = correlate(*steps[i + 1]) if i + 1 < len(steps) else None
        if i > 0:
            later = pull(*steps[i - 1], weights, later)
        if i < len(steps):
            weights = weigh(*steps[i], gram)
        gram = ahead
    back = regroup(True)
    copies = []
    for gr in range(8):
        rows = jnp.concatenate(
            [
                d_ref[r8 % KB, (r8 // KB) * WINS + gr * 32 : (r8 // KB) * WINS + gr * 32 + 32, :]
                for r8 in range(8)
            ],
            axis=0,
        )
        place = slice(gr * 256, (gr + 1) * 256)
        out_ref[place, :] = dot(back, rows).astype(BF16)
        copy = pltpu.make_async_copy(out_ref.at[place, :], out_hbm.at[place, :], sem.at[gr])
        copy.start()
        copies.append(copy)
    for copy in copies:
        copy.wait()


def middle(scalars, x, obs):
    return pl.pallas_call(
        middle_kernel,
        in_specs=[IN_SMEM, IN_VMEM, IN_VMEM],
        out_specs=[IN_VMEM, IN_HBM],
        scratch_shapes=[
            pltpu.VMEM((KB, 2 * WINS, CH), BF16),
            pltpu.VMEM((KB, 2 * WINS, CH), BF16),
            pltpu.VMEM((2048, CH), BF16),
            pltpu.SemaphoreType.DMA((8,)),
        ],
        out_shape=[
            jax.ShapeDtypeStruct((NB, 2, KB, 8, LANES), BF16),
            pltpu.HBM((2048, CH), BF16),
        ],
        compiler_params=pltpu.CompilerParams(vmem_limit_bytes=VMEM_LIMIT),
        name="middle",
    )(scalars, x, obs)


def unpack_kernel(sc_ref, up_ref, down_ref, o_ref):
    perm = regroup(False, True)
    low, me = sc_ref[5], sc_ref[6]
    regrouped = ([], [])
    for gr in range(4):
        sides = []
        for ref in (up_ref, down_ref):
            rows = [ref[source_slot(me, gr * 8 + j)].astype(F32).reshape(32, LANES) for j in range(8)]
            sides.append(jnp.concatenate(rows, axis=0))
        regrouped[0].append(dot(perm, jnp.where(low == 1, sides[1], sides[0]).astype(BF16)))
        regrouped[1].append(dot(perm, jnp.where(low == 1, sides[0], sides[1]).astype(BF16)))
    for h in range(2):
        for i in range(8):
            page = jnp.concatenate([r[i * 32 : (i + 1) * 32] for r in regrouped[h]], axis=0)
            turned = page.T
            for ih in range(2):
                for s in range(SLOTS):
                    val = jnp.zeros((CB, LANES), F32)
                    for o in range(OFFSETS):
                        row = ih * HALF + o * CB
                        val = jnp.where(sc_ref[s] == o, turned[row : row + CB], val)
                    o_ref[s, ih * 8 + i, :, h * LANES : (h + 1) * LANES] = val


def unpack_correl(scalars, up, down):
    block = lambda shape: pl.BlockSpec(shape, lambda i, sc: (0,) * len(shape))
    return pl.pallas_call(
        unpack_kernel,
        grid_spec=pltpu.PrefetchScalarGridSpec(
            num_scalar_prefetch=1,
            grid=(1,),
            in_specs=[block((NB, KB, 8, LANES))] * 2,
            out_specs=block((SLOTS, CB, CB, 2 * LANES)),
        ),
        out_shape=jax.ShapeDtypeStruct((SLOTS, CB, CB, 2 * LANES), F32),
        compiler_params=pltpu.CompilerParams(vmem_limit_bytes=VMEM_LIMIT),
        name="unpack_correl",
    )(scalars, up, down)


def on_device(traces, pair_lists, observed):
    consts = [jnp.asarray(v) for v in table_parts()]
    white, inverse = forward(traces[0], consts)
    white, pair_lists = lax.optimization_barrier((white, pair_lists))
    g, me = lax.axis_index("grp"), lax.axis_index("win")
    half, q = half_of(g), quarter_of(g)
    low = jnp.where(g < 4, 1, 0)
    scalars = jnp.concatenate([pair_lists[0], jnp.stack([2 * q + half, half, low, me]).astype(jnp.int32)])
    moved = lax.all_to_all(white.reshape(WINS, 8, CH), ("win", "grp"), 0, 0)
    seen = exchange(pack_observed(scalars, observed[0]))
    corr, grad = middle(scalars, moved.reshape(2048, CH), seen)
    returned = lax.all_to_all(grad.reshape(WINS, 8, CH), ("win", "grp"), 0, 0)
    corr = exchange(corr)
    up = lax.ppermute(corr[:, 0], "grp", [(i, (i + 1) % GRP) for i in range(GRP)])
    down = lax.ppermute(corr[:, 1], "grp", [(i, (i - 3) % GRP) for i in range(GRP)])
    trace_grad = backward(returned.reshape(16, 2, GRP, 8, CH), white, inverse, consts)
    up, down, trace_grad = lax.optimization_barrier((up, down, trace_grad))
    correl = unpack_correl(scalars, up, down)
    return correl[None], trace_grad[None]


def solution(mesh):
    return jax.shard_map(
        on_device,
        mesh=mesh,
        in_specs=(P(("win", "grp"), None, None), P("win", None), P("win", None, None, None, None)),
        out_specs=(P("win", None, None, None, "grp"), P(("win", "grp"), None, None)),
        check_vma=False,
    )
```

```python
import functools
import math

import jax
import jax.numpy as jnp
import numpy as np
from jax import lax
from jax.experimental import pallas as pl
from jax.experimental.pallas import tpu as pltpu
from jax.sharding import PartitionSpec as P

SEG = 2048
FREQ = 1024
BAND = 64
OFFSETS = 4
CB = 16
SLOTS = 3
CH = 512
WINS = 256
NB = 32
GRP = 8
KB = 4
LANES = 128
HALF = 64
EMPTY = 64.0
VMEM_LIMIT = 24 << 20

F32 = jnp.float32
BF16 = jnp.bfloat16


def half_of(g):
    return jnp.where(jnp.logical_and(g >= 3, g <= 6), 0, 1)


def quarter_of(g):
    return jnp.where(half_of(g) == 0, g - 3, (g + 1) % GRP)


def table_parts():
    row = np.arange(BAND)
    j = row // 8 * 8 + row % KB * 2
    imag = (row % 8) >= KB
    n = np.arange(SEG // 2)
    ang = 2.0 * math.pi * ((n[None, :] * j[:, None]) % SEG) / SEG
    a = np.where(imag[:, None], -np.sin(ang), np.cos(ang))
    bins = np.concatenate([BAND * np.arange(FREQ // BAND), np.ones(8, np.int64)])
    turn = 2.0 * math.pi * ((n[None, :] * bins[:, None]) % SEG) / SEG
    return [np.asarray(v, np.float32) for v in (a, np.cos(turn), np.sin(turn))]


def other_part(a):
    imag = lax.broadcasted_iota(jnp.int32, a.shape, 0) % 8 >= KB
    return jnp.where(imag, -pltpu.roll(a, KB, 0), pltpu.roll(a, BAND - KB, 0))


def band_pairs(a_ref, c_ref, s_ref, cols):
    even = a_ref[:, cols]
    turned = other_part(even)
    odd = even * c_ref[16:17, cols] + turned * s_ref[16:17, cols]
    return (even, turned), (odd, other_part(odd))


NSC = 7


def target_slot(me, w):
    return ((me + w) % 2) * 16 + ((w // 2 - me // 2 + 4) % 4) * 4 + (w // 8 - me // 8 + 4) % 4


def source_slot(me, w):
    return ((me // 8 - w // 8 + 4) % 4) * 8 + ((me // 2 - w // 2 + 4) % 4) * 2 + (me + w) % 2


def exchange(blocks, across=None):
    def hop(array, dy, dx, dc):
        pairs = []
        for w in range(NB):
            y, x, c = w // 8, w // 2 % 4, w % 2
            pairs.append((w, ((y + dy) % 4 * 4 + (x + dx) % 4) * 2 + (c + dc) % 2))
        return lax.ppermute(array, "win", pairs)

    blocks = blocks.reshape((2, 4, 4) + blocks.shape[1:])
    blocks = jnp.stack([blocks[0], hop(blocks[1], 0, 0, 1)])
    along_x = [blocks[:, 0]] + [hop(blocks[:, d], 0, d, 0) for d in range(1, 4)]
    blocks = jnp.stack(along_x)
    if across is not None:
        blocks = across(blocks)
    along_y = [blocks[:, :, 0]] + [hop(blocks[:, :, d], d, 0, 0) for d in range(1, 4)]
    return [piece.reshape((8,) + piece.shape[2:]) for piece in along_y]


def dot(x, y, cx=1, cy=0):
    return lax.dot_general(x, y, (((cx,), (cy,)), ((), ())), preferred_element_type=F32)


def regroup(inverse, bins=False):
    shape = (256, 256)
    near = lax.broadcasted_iota(jnp.int32, shape, 1 if inverse else 0)
    far = lax.broadcasted_iota(jnp.int32, shape, 0 if inverse else 1)
    c = near % 32
    if bins:
        c = c // 8 * 8 + c % 2 * KB + c % 8 // 2
    return jnp.where(c * 8 + near // 32 == far, 1.0, 0.0).astype(BF16)


def full(shape):
    return pl.BlockSpec(shape, lambda *i: (0,) * len(shape))


def plane_bands(g):
    h = 0 if 3 <= g <= 6 else 1
    q = g - 3 if h == 0 else (g + 1) % GRP
    return (q * 4 + h * 2, q * 4 + h * 2 + 1)


def forward_kernel(x_hbm, a_hbm, c_hbm, s_hbm, y_hbm, r_ref, x_ref, a_ref, c_ref, s_ref, y_ref, sem):
    pieces = [(a_hbm, a_ref), (c_hbm, c_ref), (s_hbm, s_ref)]
    for i in range(4):
        rows = slice(i * 128, (i + 1) * 128)
        pieces.append((x_hbm.at[rows, :], x_ref.at[rows, :]))
    loads = [pltpu.make_async_copy(src, dst, sem.at[4 + i]) for i, (src, dst) in enumerate(pieces)]
    for load in loads:
        load.start()
    for load in loads[:3]:
        load.wait()
    pairs = band_pairs(a_ref, c_ref, s_ref, slice(None))

    def tables(step):
        for a, b in pairs:
            parts = []
            for g in (step * 2, step * 2 + 1):
                for band in plane_bands(g):
                    parts.append((a * c_ref[band : band + 1, :] + b * s_ref[band : band + 1, :]).astype(BF16))
            yield jnp.concatenate(parts, axis=0)

    ahead = list(tables(0))
    for load in loads[3:]:
        load.wait()
    early = x_ref[:, : SEG // 2].astype(F32)
    late = x_ref[:, SEG // 2 :].astype(F32)
    halves = ((early + late).astype(BF16), (early - late).astype(BF16))
    copies = []
    for step in range(4):
        waves = [dot(ahead[p], halves[p], 1, 1) for p in range(2)]
        if step < 3:
            ahead = list(tables(step + 1))
        for gi in range(2):
            for wh in range(2):
                row = (gi * 2 + wh) * 64
                rows = [w[row : row + 64] for w in waves]
                level = jnp.sum(rows[0] * rows[0] + rows[1] * rows[1], axis=0, keepdims=True)
                inv = lax.rsqrt(level * (1.0 / BAND) + 1e-05)
                r_ref[step * 2 + gi, wh : wh + 1, :] = inv
                for p in range(2):
                    tile = (rows[p] * inv).reshape(8, 8, CH).astype(BF16)
                    y_ref[wh * 8 : (wh + 1) * 8, p, step * 2 + gi] = tile
        planes = (slice(None), slice(None), slice(step * 2, step * 2 + 2))
        copy = pltpu.make_async_copy(y_ref.at[planes], y_hbm.at[planes], sem.at[step])
        copy.start()
        copies.append(copy)
    for copy in copies:
        copy.wait()


IN_HBM = pl.BlockSpec(memory_space=pltpu.HBM)
IN_VMEM = pl.BlockSpec(memory_space=pltpu.VMEM)
IN_SMEM = pl.BlockSpec(memory_space=pltpu.SMEM)


def forward(x, consts):
    return pl.pallas_call(
        forward_kernel,
        in_specs=[IN_HBM] * 4,
        out_specs=[IN_HBM, IN_VMEM],
        out_shape=[
            pltpu.HBM((16, 2, GRP, 8, CH), BF16),
            jax.ShapeDtypeStruct((GRP, 2, CH), F32),
        ],
        scratch_shapes=[
            pltpu.VMEM((CH, SEG), BF16),
            pltpu.VMEM((BAND, SEG // 2), F32),
            pltpu.VMEM((24, SEG // 2), F32),
            pltpu.VMEM((24, SEG // 2), F32),
            pltpu.VMEM((16, 2, GRP, 8, CH), BF16),
            pltpu.SemaphoreType.DMA((11,)),
        ],
        compiler_params=pltpu.CompilerParams(vmem_limit_bytes=VMEM_LIMIT),
        cost_estimate=pl.CostEstimate(flops=CH * SEG * SEG, bytes_accessed=8 << 20, transcendentals=0),
        name="forward",
    )(*(pltpu.with_memory_space_constraint(v, pltpu.HBM) for v in (x, *consts)))


def backward_kernel(g_hbm, y_ref, r_ref, a_ref, c_ref, s_ref, o_ref, g_ref, d_ref, stage_ref, sem):
    loads = []
    for step in range(4):
        planes = (slice(None), slice(None), slice(step * 2, step * 2 + 2))
        load = pltpu.make_async_copy(g_hbm.at[planes], g_ref.at[planes], sem.at[8 + step])
        load.start()
        loads.append(load)
    for plane in range(GRP):
        if plane % 2 == 0:
            loads[plane // 2].wait()
        sides = ([], [])
        for wh in range(2):
            at = slice(wh * 8, (wh + 1) * 8)
            g = [g_ref[at, p, plane].astype(F32).reshape(64, CH) for p in range(2)]
            y = [y_ref[at, p, plane].astype(F32).reshape(64, CH) for p in range(2)]
            inv = r_ref[plane, wh : wh + 1, :]
            mean = jnp.sum(g[0] * y[0] + g[1] * y[1], axis=0, keepdims=True) * (1.0 / BAND)
            for p in range(2):
                sides[p].append((g[p] - y[p] * mean) * inv)
        for p in range(2):
            turned = jnp.concatenate(sides[p], axis=0).astype(BF16).T
            d_ref[p, :, plane * 128 : (plane + 1) * 128] = turned

    tile = 256
    tiles = SEG // 2 // tile
    copies = []
    for t in range(tiles):
        cols = slice(t * tile, (t + 1) * tile)
        pairs = band_pairs(a_ref, c_ref, s_ref, cols)
        waves = []
        for p in range(2):
            a, b = pairs[p]
            parts = []
            for plane in range(GRP):
                for band in plane_bands(plane):
                    c = c_ref[band : band + 1, cols]
                    s = s_ref[band : band + 1, cols]
                    parts.append((a * c + b * s).astype(BF16))
            waves.append(dot(d_ref[p], jnp.concatenate(parts, axis=0)))
        stage_ref[2 * t] = (waves[0] + waves[1]).astype(BF16)
        stage_ref[2 * t + 1] = (waves[0] - waves[1]).astype(BF16)
        for part in range(2):
            to = o_ref.at[:, pl.ds(part * (SEG // 2) + t * tile, tile)]
            copy = pltpu.make_async_copy(stage_ref.at[2 * t + part], to, sem.at[2 * t + part])
            copy.start()
            copies.append(copy)
    for copy in copies:
        copy.wait()


def backward(g, y, r, consts):
    return pl.pallas_call(
        backward_kernel,
        in_specs=[IN_HBM] + [IN_VMEM] * 5,
        out_specs=pl.BlockSpec(memory_space=pl.ANY),
        out_shape=jax.ShapeDtypeStruct((CH, SEG), BF16),
        scratch_shapes=[
            pltpu.VMEM((16, 2, GRP, 8, CH), BF16),
            pltpu.VMEM((2, CH, SEG // 2), BF16),
            pltpu.VMEM((8, CH, 256), BF16),
            pltpu.SemaphoreType.DMA((12,)),
        ],
        compiler_params=pltpu.CompilerParams(vmem_limit_bytes=VMEM_LIMIT),
        cost_estimate=pl.CostEstimate(flops=CH * SEG * SEG, bytes_accessed=10 << 20, transcendentals=0),
        name="backward",
    )(g, y, r, *consts)


def pack_kernel(sc_ref, re_ref, im_ref, o_ref):
    perm = regroup(True, True)
    for ri, src in enumerate((re_ref, im_ref)):
        turned = []
        for i in range(8):
            rows = []
            for ih in range(2):
                for o in range(OFFSETS):
                    val = jnp.full((CB, LANES), EMPTY, F32)
                    for s in range(SLOTS):
                        val = jnp.where(sc_ref[s] == o, src[s, ih * 8 + i], val)
                    rows.append(val)
            turned.append(jnp.concatenate(rows, axis=0).T.astype(BF16))
        for gr in range(4):
            stack = jnp.concatenate([t[gr * 32 : (gr + 1) * 32] for t in turned], axis=0)
            tile = dot(perm, stack).reshape(8, KB, 8, LANES)
            for j in range(8):
                o_ref[target_slot(sc_ref[6], gr * 8 + j), ri] = tile[j].astype(BF16)


def pack_observed(scalars, observed):
    spec = lambda base: pl.BlockSpec((SLOTS, CB, CB, LANES), lambda i, sc: (0, 0, 0, base + sc[3]))
    return pl.pallas_call(
        pack_kernel,
        grid_spec=pltpu.PrefetchScalarGridSpec(
            num_scalar_prefetch=1,
            grid=(1,),
            in_specs=[spec(0), spec(8)],
            out_specs=pl.BlockSpec((32, 2, KB, 8, LANES), lambda i, sc: (0, 0, 0, 0, 0)),
        ),
        out_shape=jax.ShapeDtypeStruct((32, 2, KB, 8, LANES), BF16),
        compiler_params=pltpu.CompilerParams(vmem_limit_bytes=VMEM_LIMIT),
        name="pack_observed",
    )(scalars, observed, observed)


def middle_kernel(sc_ref, x_ref, obs_ref, corr_ref, out_hbm, u_ref, d_ref, out_ref, sem):
    half, me = sc_ref[4], sc_ref[6]
    perm = regroup(False)
    for gr in range(8):
        y = dot(perm, x_ref[gr * 256 : (gr + 1) * 256, :]).astype(BF16)
        for r8 in range(8):
            ri, k = r8 // KB, r8 % KB
            row = ri * WINS + gr * 32
            u_ref[k, row : row + 32, :] = y[r8 * 32 : (r8 + 1) * 32]

    lane8 = lax.broadcasted_iota(jnp.int32, (8, LANES), 1)
    lane16 = lax.broadcasted_iota(jnp.int32, (16, LANES), 1)

    def correlate(k, b, width):
        cols = slice(b * LANES, (b + width) * LANES)
        lead = u_ref[k, :, b * LANES : (b + 1) * LANES]
        re_rows = u_ref[k, :WINS, cols]
        im_rows = u_ref[k, WINS:, cols]
        straight = jnp.concatenate([re_rows, im_rows], axis=0)
        crossed = jnp.concatenate([im_rows, -re_rows], axis=0)
        return dot(lead.T, jnp.concatenate([straight, crossed], axis=1))

    def weigh(k, b, width, gram):
        tiles = ([], [])
        for blk in range(8):
            a, shift = b * 8 + blk, blk * CB
            source, target = source_slot(me, a), target_slot(me, a)
            for ri in range(2):
                base = ri * width * LANES
                here = gram[shift : shift + 16, base : base + LANES]
                if shift > 0:
                    if shift > HALF and width == 2:
                        there = gram[shift : shift + 16, base + LANES : base + 2 * LANES]
                        here = jnp.where(lane16 >= shift, here, there)
                    here = pltpu.roll(here, LANES - shift, 1)
                packed = jnp.where(lane8 < HALF, here[:8], pltpu.roll(here[8:], HALF, 1))
                packed = packed * (1.0 / WINS)
                seen = obs_ref[source, ri, k].astype(F32)
                corr_ref[target, 1 - half if ri == 0 else half, k] = packed.astype(BF16)
                resid = jnp.where(seen < EMPTY / 2, packed - seen, 0.0)
                spread = jnp.concatenate([resid, pltpu.roll(resid, HALF, 1)], axis=0)
                spread = jnp.where(lane16 < HALF, spread, 0.0)
                if shift > 0:
                    spread = pltpu.roll(spread, shift, 1)
                if shift > HALF:
                    first = jnp.where(lane16 >= shift, spread, 0.0)
                    second = jnp.where(lane16 < shift, spread, 0.0)
                else:
                    first, second = spread, jnp.zeros_like(spread)
                tiles[ri].append([first, second][:width])
        res = [
            [jnp.concatenate([t[p] for t in tiles[ri]], axis=0).astype(BF16) for p in range(width)]
            for ri in range(2)
        ]
        top = jnp.concatenate([m for p in range(width) for m in (res[0][p], res[1][p])], axis=1)
        low = jnp.concatenate([m for p in range(width) for m in (-res[1][p], res[0][p])], axis=1)
        return jnp.concatenate([top, low], axis=0)

    def pull(k, b, width, weights, later):
        waves = [
            u_ref[k, ri * WINS : (ri + 1) * WINS, (b + p) * LANES : (b + p + 1) * LANES]
            for p in range(width)
            for ri in range(2)
        ]
        pushed = dot(jnp.concatenate(waves[:2], axis=1), weights)
        grad = dot(jnp.concatenate(waves, axis=1), weights, 1, 1) + pushed[:, :256]
        if b > 0:
            grad = grad + later
        d_ref[k, :WINS, b * LANES : (b + 1) * LANES] = grad[:, :LANES].astype(BF16)
        d_ref[k, WINS:, b * LANES : (b + 1) * LANES] = grad[:, LANES:].astype(BF16)
        return pushed[:, 256:]

    steps = [(k, b, 2 if b < 3 else 1) for k in range(KB) for b in range(4)]
    gram, weights, later = correlate(*steps[0]), None, None
    for i in range(len(steps) + 1):
        ahead = correlate(*steps[i + 1]) if i + 1 < len(steps) else None
        if i > 0:
            later = pull(*steps[i - 1], weights, later)
        if i < len(steps):
            weights = weigh(*steps[i], gram)
        gram = ahead
    back = regroup(True)
    copies = []
    for gr in range(8):
        rows = jnp.concatenate(
            [
                d_ref[r8 % KB, (r8 // KB) * WINS + gr * 32 : (r8 // KB) * WINS + gr * 32 + 32, :]
                for r8 in range(8)
            ],
            axis=0,
        )
        place = slice(gr * 256, (gr + 1) * 256)
        out_ref[place, :] = dot(back, rows).astype(BF16)
        copy = pltpu.make_async_copy(out_ref.at[place, :], out_hbm.at[place, :], sem.at[gr])
        copy.start()
        copies.append(copy)
    for copy in copies:
        copy.wait()


def middle(scalars, x, obs):
    return pl.pallas_call(
        middle_kernel,
        in_specs=[IN_SMEM, IN_VMEM, IN_VMEM],
        out_specs=[IN_VMEM, IN_HBM],
        scratch_shapes=[
            pltpu.VMEM((KB, 2 * WINS, CH), BF16),
            pltpu.VMEM((KB, 2 * WINS, CH), BF16),
            pltpu.VMEM((2048, CH), BF16),
            pltpu.SemaphoreType.DMA((8,)),
        ],
        out_shape=[
            jax.ShapeDtypeStruct((NB, 2, KB, 8, LANES), BF16),
            pltpu.HBM((2048, CH), BF16),
        ],
        compiler_params=pltpu.CompilerParams(vmem_limit_bytes=VMEM_LIMIT),
        name="middle",
    )(scalars, x, obs)


def unpack_kernel(sc_ref, *refs):
    *pieces, o_ref, x_ref = refs
    for i, piece in enumerate(pieces):
        x_ref[i * 8 : (i + 1) * 8] = piece[...]
    perm = regroup(False, True)
    low, me = sc_ref[5], sc_ref[6]
    regrouped = ([], [])
    for gr in range(4):
        sides = []
        for side in range(2):
            rows = [x_ref[source_slot(me, gr * 8 + j), side].astype(F32).reshape(32, LANES) for j in range(8)]
            sides.append(jnp.concatenate(rows, axis=0))
        regrouped[0].append(dot(perm, jnp.where(low == 1, sides[1], sides[0]).astype(BF16)))
        regrouped[1].append(dot(perm, jnp.where(low == 1, sides[0], sides[1]).astype(BF16)))
    for h in range(2):
        for i in range(8):
            page = jnp.concatenate([r[i * 32 : (i + 1) * 32] for r in regrouped[h]], axis=0)
            turned = page.T
            for ih in range(2):
                for s in range(SLOTS):
                    val = jnp.zeros((CB, LANES), F32)
                    for o in range(OFFSETS):
                        row = ih * HALF + o * CB
                        val = jnp.where(sc_ref[s] == o, turned[row : row + CB], val)
                    o_ref[s, ih * 8 + i, :, h * LANES : (h + 1) * LANES] = val


def unpack_correl(scalars, pieces):
    block = lambda shape: pl.BlockSpec(shape, lambda i, sc: (0,) * len(shape))
    return pl.pallas_call(
        unpack_kernel,
        grid_spec=pltpu.PrefetchScalarGridSpec(
            num_scalar_prefetch=1,
            grid=(1,),
            in_specs=[block((8, 2, KB, 8, LANES))] * 4,
            out_specs=block((SLOTS, CB, CB, 2 * LANES)),
            scratch_shapes=[pltpu.VMEM((NB, 2, KB, 8, LANES), BF16)],
        ),
        out_shape=jax.ShapeDtypeStruct((SLOTS, CB, CB, 2 * LANES), F32),
        compiler_params=pltpu.CompilerParams(vmem_limit_bytes=VMEM_LIMIT),
        name="unpack_correl",
    )(scalars, *pieces)


def on_device(traces, pair_lists, observed):
    consts = [jnp.asarray(v) for v in table_parts()]
    white, inverse = forward(traces[0], consts)
    white, pair_lists = lax.optimization_barrier((white, pair_lists))
    g, me = lax.axis_index("grp"), lax.axis_index("win")
    half, q = half_of(g), quarter_of(g)
    low = jnp.where(g < 4, 1, 0)
    scalars = jnp.concatenate([pair_lists[0], jnp.stack([2 * q + half, half, low, me]).astype(jnp.int32)])
    moved = lax.all_to_all(white.reshape(WINS, 8, CH), ("win", "grp"), 0, 0)
    seen = jnp.concatenate(exchange(pack_observed(scalars, observed[0])))
    corr, grad = middle(scalars, moved.reshape(2048, CH), seen)
    returned = lax.all_to_all(grad.reshape(WINS, 8, CH), ("win", "grp"), 0, 0)

    def across(blocks):
        up = lax.ppermute(blocks[..., 0, :, :, :], "grp", [(i, (i + 1) % GRP) for i in range(GRP)])
        down = lax.ppermute(blocks[..., 1, :, :, :], "grp", [(i, (i - 3) % GRP) for i in range(GRP)])
        return jnp.stack([up, down], axis=-4)

    owned = exchange(corr, across)
    trace_grad = backward(returned.reshape(16, 2, GRP, 8, CH), white, inverse, consts)
    owned, trace_grad = lax.optimization_barrier((owned, trace_grad))
    correl = unpack_correl(scalars, owned)
    return correl[None], trace_grad[None]


def solution(mesh):
    return jax.shard_map(
        on_device,
        mesh=mesh,
        in_specs=(P(("win", "grp"), None, None), P("win", None), P("win", None, None, None, None)),
        out_specs=(P("win", None, None, None, "grp"), P(("win", "grp"), None, None)),
        check_vma=False,
    )
```

```python
import functools
import math

import jax
import jax.numpy as jnp
import numpy as np
from jax import lax
from jax.experimental import pallas as pl
from jax.experimental.pallas import tpu as pltpu
from jax.sharding import PartitionSpec as P

SEG = 2048
FREQ = 1024
BAND = 64
OFFSETS = 4
CB = 16
SLOTS = 3
CH = 512
WINS = 256
NB = 32
GRP = 8
KB = 4
LANES = 128
HALF = 64
EMPTY = 64.0
VMEM_LIMIT = 24 << 20

F32 = jnp.float32
BF16 = jnp.bfloat16


def half_of(g):
    return jnp.where(jnp.logical_and(g >= 1, g <= 4), 1, 0)


def quarter_of(g):
    return jnp.where(half_of(g) == 1, g - 1, (g + 3) % GRP)


def table_parts():
    row = np.arange(BAND)
    j = row // 8 * 8 + row % KB * 2
    imag = (row % 8) >= KB
    n = np.arange(SEG // 2)
    ang = 2.0 * math.pi * ((n[None, :] * j[:, None]) % SEG) / SEG
    a = np.where(imag[:, None], -np.sin(ang), np.cos(ang))
    bins = np.concatenate([BAND * np.arange(FREQ // BAND), np.ones(8, np.int64)])
    turn = 2.0 * math.pi * ((n[None, :] * bins[:, None]) % SEG) / SEG
    return [np.asarray(v, np.float32) for v in (a, np.cos(turn), np.sin(turn))]


def other_part(a):
    imag = lax.broadcasted_iota(jnp.int32, a.shape, 0) % 8 >= KB
    return jnp.where(imag, -pltpu.roll(a, KB, 0), pltpu.roll(a, BAND - KB, 0))


def band_pairs(a_ref, c_ref, s_ref, cols):
    even = a_ref[:, cols]
    turned = other_part(even)
    odd = even * c_ref[16:17, cols] + turned * s_ref[16:17, cols]
    return (even, turned), (odd, other_part(odd))


NSC = 7


def target_slot(me, w):
    return ((me + w) % 2) * 16 + ((w // 2 - me // 2 + 4) % 4) * 4 + (w // 8 - me // 8 + 4) % 4


def source_slot(me, w):
    return ((me // 8 - w // 8 + 4) % 4) * 8 + ((me // 2 - w // 2 + 4) % 4) * 2 + (me + w) % 2


def exchange(blocks):
    def hop(array, dy, dx, dc):
        pairs = []
        for w in range(NB):
            y, x, c = w // 8, w // 2 % 4, w % 2
            pairs.append((w, ((y + dy) % 4 * 4 + (x + dx) % 4) * 2 + (c + dc) % 2))
        return lax.ppermute(array, "win", pairs)

    blocks = blocks.reshape((2, 4, 4) + blocks.shape[1:])
    blocks = jnp.stack([blocks[0], hop(blocks[1], 0, 0, 1)])
    along_x = [blocks[:, 0]] + [hop(blocks[:, d], 0, d, 0) for d in range(1, 4)]
    blocks = jnp.stack(along_x)
    along_y = [blocks[:, :, 0]] + [hop(blocks[:, :, d], d, 0, 0) for d in range(1, 4)]
    blocks = jnp.stack(along_y)
    return blocks.reshape((NB,) + blocks.shape[3:])


def dot(x, y, cx=1, cy=0):
    return lax.dot_general(x, y, (((cx,), (cy,)), ((), ())), preferred_element_type=F32)


def regroup(inverse, bins=False):
    shape = (256, 256)
    near = lax.broadcasted_iota(jnp.int32, shape, 1 if inverse else 0)
    far = lax.broadcasted_iota(jnp.int32, shape, 0 if inverse else 1)
    c = near % 32
    if bins:
        c = c // 8 * 8 + c % 2 * KB + c % 8 // 2
    return jnp.where(c * 8 + near // 32 == far, 1.0, 0.0).astype(BF16)


def full(shape):
    return pl.BlockSpec(shape, lambda *i: (0,) * len(shape))


def plane_bands(g):
    h = 1 if 1 <= g <= 4 else 0
    q = g - 1 if h == 1 else (g + 3) % GRP
    return (q * 4 + h * 2, q * 4 + h * 2 + 1)


def forward_kernel(x_hbm, a_hbm, c_hbm, s_hbm, y_hbm, r_ref, x_ref, a_ref, c_ref, s_ref, y_ref, sem):
    pieces = [(a_hbm, a_ref), (c_hbm, c_ref), (s_hbm, s_ref)]
    for i in range(4):
        rows = slice(i * 128, (i + 1) * 128)
        pieces.append((x_hbm.at[rows, :], x_ref.at[rows, :]))
    loads = [pltpu.make_async_copy(src, dst, sem.at[4 + i]) for i, (src, dst) in enumerate(pieces)]
    for load in loads:
        load.start()
    for load in loads[:3]:
        load.wait()
    pairs = band_pairs(a_ref, c_ref, s_ref, slice(None))

    def tables(step):
        for a, b in pairs:
            parts = []
            for g in (step * 2, step * 2 + 1):
                for band in plane_bands(g):
                    parts.append((a * c_ref[band : band + 1, :] + b * s_ref[band : band + 1, :]).astype(BF16))
            yield jnp.concatenate(parts, axis=0)

    ahead = list(tables(0))
    for load in loads[3:]:
        load.wait()
    early = x_ref[:, : SEG // 2].astype(F32)
    late = x_ref[:, SEG // 2 :].astype(F32)
    halves = ((early + late).astype(BF16), (early - late).astype(BF16))
    copies = []
    for step in range(4):
        waves = [dot(ahead[p], halves[p], 1, 1) for p in range(2)]
        if step < 3:
            ahead = list(tables(step + 1))
        for gi in range(2):
            for wh in range(2):
                row = (gi * 2 + wh) * 64
                rows = [w[row : row + 64] for w in waves]
                level = jnp.sum(rows[0] * rows[0] + rows[1] * rows[1], axis=0, keepdims=True)
                inv = lax.rsqrt(level * (1.0 / BAND) + 1e-05)
                r_ref[step * 2 + gi, wh : wh + 1, :] = inv
                for p in range(2):
                    tile = (rows[p] * inv).reshape(8, 8, CH).astype(BF16)
                    y_ref[wh * 8 : (wh + 1) * 8, p, step * 2 + gi] = tile
        planes = (slice(None), slice(None), slice(step * 2, step * 2 + 2))
        copy = pltpu.make_async_copy(y_ref.at[planes], y_hbm.at[planes], sem.at[step])
        copy.start()
        copies.append(copy)
    for copy in copies:
        copy.wait()


IN_HBM = pl.BlockSpec(memory_space=pltpu.HBM)
IN_VMEM = pl.BlockSpec(memory_space=pltpu.VMEM)
IN_SMEM = pl.BlockSpec(memory_space=pltpu.SMEM)


def forward(x, consts):
    return pl.pallas_call(
        forward_kernel,
        in_specs=[IN_HBM] * 4,
        out_specs=[IN_HBM, IN_VMEM],
        out_shape=[
            pltpu.HBM((16, 2, GRP, 8, CH), BF16),
            jax.ShapeDtypeStruct((GRP, 2, CH), F32),
        ],
        scratch_shapes=[
            pltpu.VMEM((CH, SEG), BF16),
            pltpu.VMEM((BAND, SEG // 2), F32),
            pltpu.VMEM((24, SEG // 2), F32),
            pltpu.VMEM((24, SEG // 2), F32),
            pltpu.VMEM((16, 2, GRP, 8, CH), BF16),
            pltpu.SemaphoreType.DMA((11,)),
        ],
        compiler_params=pltpu.CompilerParams(vmem_limit_bytes=VMEM_LIMIT),
        cost_estimate=pl.CostEstimate(flops=CH * SEG * SEG, bytes_accessed=8 << 20, transcendentals=0),
        name="forward",
    )(*(pltpu.with_memory_space_constraint(v, pltpu.HBM) for v in (x, *consts)))


def backward_kernel(g_hbm, y_ref, r_ref, a_ref, c_ref, s_ref, o_ref, g_ref, d_ref, stage_ref, sem):
    loads = []
    for step in range(4):
        planes = (slice(None), slice(None), slice(step * 2, step * 2 + 2))
        load = pltpu.make_async_copy(g_hbm.at[planes], g_ref.at[planes], sem.at[8 + step])
        load.start()
        loads.append(load)
    for plane in range(GRP):
        if plane % 2 == 0:
            loads[plane // 2].wait()
        sides = ([], [])
        for wh in range(2):
            at = slice(wh * 8, (wh + 1) * 8)
            g = [g_ref[at, p, plane].astype(F32).reshape(64, CH) for p in range(2)]
            y = [y_ref[at, p, plane].astype(F32).reshape(64, CH) for p in range(2)]
            inv = r_ref[plane, wh : wh + 1, :]
            mean = jnp.sum(g[0] * y[0] + g[1] * y[1], axis=0, keepdims=True) * (1.0 / BAND)
            for p in range(2):
                sides[p].append((g[p] - y[p] * mean) * inv)
        for p in range(2):
            turned = jnp.concatenate(sides[p], axis=0).astype(BF16).T
            d_ref[p, :, plane * 128 : (plane + 1) * 128] = turned

    tile = 256
    tiles = SEG // 2 // tile
    copies = []
    for t in range(tiles):
        cols = slice(t * tile, (t + 1) * tile)
        pairs = band_pairs(a_ref, c_ref, s_ref, cols)
        waves = []
        for p in range(2):
            a, b = pairs[p]
            parts = []
            for plane in range(GRP):
                for band in plane_bands(plane):
                    c = c_ref[band : band + 1, cols]
                    s = s_ref[band : band + 1, cols]
                    parts.append((a * c + b * s).astype(BF16))
            waves.append(dot(d_ref[p], jnp.concatenate(parts, axis=0)))
        stage_ref[2 * t] = (waves[0] + waves[1]).astype(BF16)
        stage_ref[2 * t + 1] = (waves[0] - waves[1]).astype(BF16)
        for part in range(2):
            to = o_ref.at[:, pl.ds(part * (SEG // 2) + t * tile, tile)]
            copy = pltpu.make_async_copy(stage_ref.at[2 * t + part], to, sem.at[2 * t + part])
            copy.start()
            copies.append(copy)
    for copy in copies:
        copy.wait()


def backward(g, y, r, consts):
    return pl.pallas_call(
        backward_kernel,
        in_specs=[IN_HBM] + [IN_VMEM] * 5,
        out_specs=pl.BlockSpec(memory_space=pl.ANY),
        out_shape=jax.ShapeDtypeStruct((CH, SEG), BF16),
        scratch_shapes=[
            pltpu.VMEM((16, 2, GRP, 8, CH), BF16),
            pltpu.VMEM((2, CH, SEG // 2), BF16),
            pltpu.VMEM((8, CH, 256), BF16),
            pltpu.SemaphoreType.DMA((12,)),
        ],
        compiler_params=pltpu.CompilerParams(vmem_limit_bytes=VMEM_LIMIT),
        cost_estimate=pl.CostEstimate(flops=CH * SEG * SEG, bytes_accessed=10 << 20, transcendentals=0),
        name="backward",
    )(g, y, r, *consts)


def pack_kernel(sc_ref, re_ref, im_ref, o_ref):
    perm = regroup(True, True)
    for ri, src in enumerate((re_ref, im_ref)):
        turned = []
        for i in range(8):
            rows = []
            for ih in range(2):
                for o in range(OFFSETS):
                    val = jnp.full((CB, LANES), EMPTY, F32)
                    for s in range(SLOTS):
                        val = jnp.where(sc_ref[s] == o, src[s, ih * 8 + i], val)
                    rows.append(val)
            turned.append(jnp.concatenate(rows, axis=0).T.astype(BF16))
        for gr in range(4):
            stack = jnp.concatenate([t[gr * 32 : (gr + 1) * 32] for t in turned], axis=0)
            tile = dot(perm, stack).reshape(8, KB, 8, LANES)
            for j in range(8):
                o_ref[target_slot(sc_ref[6], gr * 8 + j), ri] = tile[j].astype(BF16)


def pack_observed(scalars, observed):
    spec = lambda base: pl.BlockSpec((SLOTS, CB, CB, LANES), lambda i, sc: (0, 0, 0, base + sc[3]))
    return pl.pallas_call(
        pack_kernel,
        grid_spec=pltpu.PrefetchScalarGridSpec(
            num_scalar_prefetch=1,
            grid=(1,),
            in_specs=[spec(0), spec(8)],
            out_specs=pl.BlockSpec((32, 2, KB, 8, LANES), lambda i, sc: (0, 0, 0, 0, 0)),
        ),
        out_shape=jax.ShapeDtypeStruct((32, 2, KB, 8, LANES), BF16),
        compiler_params=pltpu.CompilerParams(vmem_limit_bytes=VMEM_LIMIT),
        name="pack_observed",
    )(scalars, observed, observed)


def middle_kernel(sc_ref, x_ref, obs_ref, corr_ref, out_hbm, u_ref, d_ref, out_ref, sem):
    half, me = sc_ref[4], sc_ref[6]
    perm = regroup(False)
    for gr in range(8):
        y = dot(perm, x_ref[gr * 256 : (gr + 1) * 256, :]).astype(BF16)
        for r8 in range(8):
            ri, k = r8 // KB, r8 % KB
            row = ri * WINS + gr * 32
            u_ref[k, row : row + 32, :] = y[r8 * 32 : (r8 + 1) * 32]

    lane8 = lax.broadcasted_iota(jnp.int32, (8, LANES), 1)
    lane16 = lax.broadcasted_iota(jnp.int32, (16, LANES), 1)

    def correlate(k, b, width):
        cols = slice(b * LANES, (b + width) * LANES)
        lead = u_ref[k, :, b * LANES : (b + 1) * LANES]
        re_rows = u_ref[k, :WINS, cols]
        im_rows = u_ref[k, WINS:, cols]
        straight = jnp.concatenate([re_rows, im_rows], axis=0)
        crossed = jnp.concatenate([im_rows, -re_rows], axis=0)
        return dot(lead.T, jnp.concatenate([straight, crossed], axis=1))

    def weigh(k, b, width, gram):
        tiles = ([], [])
        for blk in range(8):
            a, shift = b * 8 + blk, blk * CB
            source, target = source_slot(me, a), target_slot(me, a)
            for ri in range(2):
                base = ri * width * LANES
                here = gram[shift : shift + 16, base : base + LANES]
                if shift > 0:
                    if shift > HALF and width == 2:
                        there = gram[shift : shift + 16, base + LANES : base + 2 * LANES]
                        here = jnp.where(lane16 >= shift, here, there)
                    here = pltpu.roll(here, LANES - shift, 1)
                packed = jnp.where(lane8 < HALF, here[:8], pltpu.roll(here[8:], HALF, 1))
                packed = packed * (1.0 / WINS)
                seen = obs_ref[source, ri, k].astype(F32)
                corr_ref[target, 1 - half if ri == 0 else half, k] = packed.astype(BF16)
                resid = jnp.where(seen < EMPTY / 2, packed - seen, 0.0)
                spread = jnp.concatenate([resid, pltpu.roll(resid, HALF, 1)], axis=0)
                spread = jnp.where(lane16 < HALF, spread, 0.0)
                if shift > 0:
                    spread = pltpu.roll(spread, shift, 1)
                if shift > HALF:
                    first = jnp.where(lane16 >= shift, spread, 0.0)
                    second = jnp.where(lane16 < shift, spread, 0.0)
                else:
                    first, second = spread, jnp.zeros_like(spread)
                tiles[ri].append([first, second][:width])
        res = [
            [jnp.concatenate([t[p] for t in tiles[ri]], axis=0).astype(BF16) for p in range(width)]
            for ri in range(2)
        ]
        top = jnp.concatenate([m for p in range(width) for m in (res[0][p], res[1][p])], axis=1)
        low = jnp.concatenate([m for p in range(width) for m in (-res[1][p], res[0][p])], axis=1)
        return jnp.concatenate([top, low], axis=0)

    def pull(k, b, width, weights, later):
        waves = [
            u_ref[k, ri * WINS : (ri + 1) * WINS, (b + p) * LANES : (b + p + 1) * LANES]
            for p in range(width)
            for ri in range(2)
        ]
        pushed = dot(jnp.concatenate(waves[:2], axis=1), weights)
        grad = dot(jnp.concatenate(waves, axis=1), weights, 1, 1) + pushed[:, :256]
        if b > 0:
            grad = grad + later
        d_ref[k, :WINS, b * LANES : (b + 1) * LANES] = grad[:, :LANES].astype(BF16)
        d_ref[k, WINS:, b * LANES : (b + 1) * LANES] = grad[:, LANES:].astype(BF16)
        return pushed[:, 256:]

    steps = [(k, b, 2 if b < 3 else 1) for k in range(KB) for b in range(4)]
    gram, weights, later = correlate(*steps[0]), None, None
    for i in range(len(steps) + 1):
        ahead = correlate(*steps[i + 1]) if i + 1 < len(steps) else None
        if i > 0:
            later = pull(*steps[i - 1], weights, later)
        if i < len(steps):
            weights = weigh(*steps[i], gram)
        gram = ahead
    back = regroup(True)
    copies = []
    for gr in range(8):
        rows = jnp.concatenate(
            [
                d_ref[r8 % KB, (r8 // KB) * WINS + gr * 32 : (r8 // KB) * WINS + gr * 32 + 32, :]
                for r8 in range(8)
            ],
            axis=0,
        )
        place = slice(gr * 256, (gr + 1) * 256)
        out_ref[place, :] = dot(back, rows).astype(BF16)
        copy = pltpu.make_async_copy(out_ref.at[place, :], out_hbm.at[place, :], sem.at[gr])
        copy.start()
        copies.append(copy)
    for copy in copies:
        copy.wait()


def middle(scalars, x, obs):
    return pl.pallas_call(
        middle_kernel,
        in_specs=[IN_SMEM, IN_VMEM, IN_VMEM],
        out_specs=[IN_VMEM, IN_HBM],
        scratch_shapes=[
            pltpu.VMEM((KB, 2 * WINS, CH), BF16),
            pltpu.VMEM((KB, 2 * WINS, CH), BF16),
            pltpu.VMEM((2048, CH), BF16),
            pltpu.SemaphoreType.DMA((8,)),
        ],
        out_shape=[
            jax.ShapeDtypeStruct((NB, 2, KB, 8, LANES), BF16),
            pltpu.HBM((2048, CH), BF16),
        ],
        compiler_params=pltpu.CompilerParams(vmem_limit_bytes=VMEM_LIMIT),
        name="middle",
    )(scalars, x, obs)


def unpack_kernel(sc_ref, up_ref, down_ref, o_ref):
    perm = regroup(False, True)
    low, me = sc_ref[5], sc_ref[6]
    regrouped = ([], [])
    for gr in range(4):
        sides = []
        for ref in (up_ref, down_ref):
            rows = [ref[source_slot(me, gr * 8 + j)].astype(F32).reshape(32, LANES) for j in range(8)]
            sides.append(jnp.concatenate(rows, axis=0))
        regrouped[0].append(dot(perm, jnp.where(low == 1, sides[1], sides[0]).astype(BF16)))
        regrouped[1].append(dot(perm, jnp.where(low == 1, sides[0], sides[1]).astype(BF16)))
    for h in range(2):
        for i in range(8):
            page = jnp.concatenate([r[i * 32 : (i + 1) * 32] for r in regrouped[h]], axis=0)
            turned = page.T
            for ih in range(2):
                for s in range(SLOTS):
                    val = jnp.zeros((CB, LANES), F32)
                    for o in range(OFFSETS):
                        row = ih * HALF + o * CB
                        val = jnp.where(sc_ref[s] == o, turned[row : row + CB], val)
                    o_ref[s, ih * 8 + i, :, h * LANES : (h + 1) * LANES] = val


def unpack_correl(scalars, up, down):
    block = lambda shape: pl.BlockSpec(shape, lambda i, sc: (0,) * len(shape))
    return pl.pallas_call(
        unpack_kernel,
        grid_spec=pltpu.PrefetchScalarGridSpec(
            num_scalar_prefetch=1,
            grid=(1,),
            in_specs=[block((NB, KB, 8, LANES))] * 2,
            out_specs=block((SLOTS, CB, CB, 2 * LANES)),
        ),
        out_shape=jax.ShapeDtypeStruct((SLOTS, CB, CB, 2 * LANES), F32),
        compiler_params=pltpu.CompilerParams(vmem_limit_bytes=VMEM_LIMIT),
        name="unpack_correl",
    )(scalars, up, down)


def on_device(traces, pair_lists, observed):
    consts = [jnp.asarray(v) for v in table_parts()]
    white, inverse = forward(traces[0], consts)
    white, pair_lists = lax.optimization_barrier((white, pair_lists))
    g, me = lax.axis_index("grp"), lax.axis_index("win")
    half, q = half_of(g), quarter_of(g)
    low = jnp.where(g < 4, 1, 0)
    scalars = jnp.concatenate([pair_lists[0], jnp.stack([2 * q + half, half, low, me]).astype(jnp.int32)])
    moved = lax.all_to_all(white.reshape(WINS, 8, CH), ("win", "grp"), 0, 0)
    seen = exchange(pack_observed(scalars, observed[0]))
    corr, grad = middle(scalars, moved.reshape(2048, CH), seen)
    returned = lax.all_to_all(grad.reshape(WINS, 8, CH), ("win", "grp"), 0, 0)
    corr = exchange(corr)
    up = lax.ppermute(corr[:, 0], "grp", [(i, (i - 1) % GRP) for i in range(GRP)])
    down = lax.ppermute(corr[:, 1], "grp", [(i, (i + 3) % GRP) for i in range(GRP)])
    trace_grad = backward(returned.reshape(16, 2, GRP, 8, CH), white, inverse, consts)
    up, down, trace_grad = lax.optimization_barrier((up, down, trace_grad))
    correl = unpack_correl(scalars, up, down)
    return correl[None], trace_grad[None]


def solution(mesh):
    return jax.shard_map(
        on_device,
        mesh=mesh,
        in_specs=(P(("win", "grp"), None, None), P("win", None), P("win", None, None, None, None)),
        out_specs=(P("win", None, None, None, "grp"), P(("win", "grp"), None, None)),
        check_vma=False,
    )
```

```python
import functools
import math

import jax
import jax.numpy as jnp
import numpy as np
from jax import lax
from jax.experimental import pallas as pl
from jax.experimental.pallas import tpu as pltpu
from jax.sharding import PartitionSpec as P

SEG = 2048
FREQ = 1024
BAND = 64
OFFSETS = 4
CB = 16
SLOTS = 3
CH = 512
WINS = 256
NB = 32
GRP = 8
KB = 4
LANES = 128
HALF = 64
EMPTY = 64.0
VMEM_LIMIT = 24 << 20

F32 = jnp.float32
BF16 = jnp.bfloat16


def half_of(g):
    return jnp.where(jnp.logical_and(g >= 2, g <= 5), 0, 1)


def quarter_of(g):
    return jnp.where(half_of(g) == 0, g - 2, (g + 2) % GRP)


def table_parts():
    row = np.arange(BAND)
    j = row // 8 * 8 + row % KB * 2
    imag = (row % 8) >= KB
    n = np.arange(SEG // 2)
    ang = 2.0 * math.pi * ((n[None, :] * j[:, None]) % SEG) / SEG
    a = np.where(imag[:, None], -np.sin(ang), np.cos(ang))
    bins = np.concatenate([BAND * np.arange(FREQ // BAND), np.ones(8, np.int64)])
    turn = 2.0 * math.pi * ((n[None, :] * bins[:, None]) % SEG) / SEG
    return [np.asarray(v, np.float32) for v in (a, np.cos(turn), np.sin(turn))]


def other_part(a):
    imag = lax.broadcasted_iota(jnp.int32, a.shape, 0) % 8 >= KB
    return jnp.where(imag, -pltpu.roll(a, KB, 0), pltpu.roll(a, BAND - KB, 0))


def band_pairs(a_ref, c_ref, s_ref, cols):
    even = a_ref[:, cols]
    turned = other_part(even)
    odd = even * c_ref[16:17, cols] + turned * s_ref[16:17, cols]
    return (even, turned), (odd, other_part(odd))


NSC = 7


def target_slot(me, w):
    return ((me + w) % 2) * 16 + ((w // 2 - me // 2 + 4) % 4) * 4 + (w // 8 - me // 8 + 4) % 4


def source_slot(me, w):
    return ((me // 8 - w // 8 + 4) % 4) * 8 + ((me // 2 - w // 2 + 4) % 4) * 2 + (me + w) % 2


def exchange(blocks):
    def hop(array, dy, dx, dc):
        pairs = []
        for w in range(NB):
            y, x, c = w // 8, w // 2 % 4, w % 2
            pairs.append((w, ((y + dy) % 4 * 4 + (x + dx) % 4) * 2 + (c + dc) % 2))
        return lax.ppermute(array, "win", pairs)

    blocks = blocks.reshape((2, 4, 4) + blocks.shape[1:])
    blocks = jnp.stack([blocks[0], hop(blocks[1], 0, 0, 1)])
    along_x = [blocks[:, 0]] + [hop(blocks[:, d], 0, d, 0) for d in range(1, 4)]
    blocks = jnp.stack(along_x)
    along_y = [blocks[:, :, 0]] + [hop(blocks[:, :, d], d, 0, 0) for d in range(1, 4)]
    blocks = jnp.stack(along_y)
    return blocks.reshape((NB,) + blocks.shape[3:])


def dot(x, y, cx=1, cy=0):
    return lax.dot_general(x, y, (((cx,), (cy,)), ((), ())), preferred_element_type=F32)


def regroup(inverse, bins=False):
    shape = (256, 256)
    near = lax.broadcasted_iota(jnp.int32, shape, 1 if inverse else 0)
    far = lax.broadcasted_iota(jnp.int32, shape, 0 if inverse else 1)
    c = near % 32
    if bins:
        c = c // 8 * 8 + c % 2 * KB + c % 8 // 2
    return jnp.where(c * 8 + near // 32 == far, 1.0, 0.0).astype(BF16)


def full(shape):
    return pl.BlockSpec(shape, lambda *i: (0,) * len(shape))


def plane_bands(g):
    h = 0 if 2 <= g <= 5 else 1
    q = g - 2 if h == 0 else (g + 2) % GRP
    return (q * 4 + h * 2, q * 4 + h * 2 + 1)


def forward_kernel(x_hbm, a_hbm, c_hbm, s_hbm, y_hbm, r_ref, x_ref, a_ref, c_ref, s_ref, y_ref, sem):
    pieces = [(a_hbm, a_ref), (c_hbm, c_ref), (s_hbm, s_ref)]
    for i in range(4):
        rows = slice(i * 128, (i + 1) * 128)
        pieces.append((x_hbm.at[rows, :], x_ref.at[rows, :]))
    loads = [pltpu.make_async_copy(src, dst, sem.at[4 + i]) for i, (src, dst) in enumerate(pieces)]
    for load in loads:
        load.start()
    for load in loads[:3]:
        load.wait()
    pairs = band_pairs(a_ref, c_ref, s_ref, slice(None))

    def tables(step):
        for a, b in pairs:
            parts = []
            for g in (step * 2, step * 2 + 1):
                for band in plane_bands(g):
                    parts.append((a * c_ref[band : band + 1, :] + b * s_ref[band : band + 1, :]).astype(BF16))
            yield jnp.concatenate(parts, axis=0)

    ahead = list(tables(0))
    for load in loads[3:]:
        load.wait()
    early = x_ref[:, : SEG // 2].astype(F32)
    late = x_ref[:, SEG // 2 :].astype(F32)
    halves = ((early + late).astype(BF16), (early - late).astype(BF16))
    copies = []
    for step in range(4):
        waves = [dot(ahead[p], halves[p], 1, 1) for p in range(2)]
        if step < 3:
            ahead = list(tables(step + 1))
        for gi in range(2):
            for wh in range(2):
                row = (gi * 2 + wh) * 64
                rows = [w[row : row + 64] for w in waves]
                level = jnp.sum(rows[0] * rows[0] + rows[1] * rows[1], axis=0, keepdims=True)
                inv = lax.rsqrt(level * (1.0 / BAND) + 1e-05)
                r_ref[step * 2 + gi, wh : wh + 1, :] = inv
                for p in range(2):
                    tile = (rows[p] * inv).reshape(8, 8, CH).astype(BF16)
                    y_ref[wh * 8 : (wh + 1) * 8, p, step * 2 + gi] = tile
        planes = (slice(None), slice(None), slice(step * 2, step * 2 + 2))
        copy = pltpu.make_async_copy(y_ref.at[planes], y_hbm.at[planes], sem.at[step])
        copy.start()
        copies.append(copy)
    for copy in copies:
        copy.wait()


IN_HBM = pl.BlockSpec(memory_space=pltpu.HBM)
IN_VMEM = pl.BlockSpec(memory_space=pltpu.VMEM)
IN_SMEM = pl.BlockSpec(memory_space=pltpu.SMEM)


def forward(x, consts):
    return pl.pallas_call(
        forward_kernel,
        in_specs=[IN_HBM] * 4,
        out_specs=[IN_HBM, IN_VMEM],
        out_shape=[
            pltpu.HBM((16, 2, GRP, 8, CH), BF16),
            jax.ShapeDtypeStruct((GRP, 2, CH), F32),
        ],
        scratch_shapes=[
            pltpu.VMEM((CH, SEG), BF16),
            pltpu.VMEM((BAND, SEG // 2), F32),
            pltpu.VMEM((24, SEG // 2), F32),
            pltpu.VMEM((24, SEG // 2), F32),
            pltpu.VMEM((16, 2, GRP, 8, CH), BF16),
            pltpu.SemaphoreType.DMA((11,)),
        ],
        compiler_params=pltpu.CompilerParams(vmem_limit_bytes=VMEM_LIMIT),
        cost_estimate=pl.CostEstimate(flops=CH * SEG * SEG, bytes_accessed=8 << 20, transcendentals=0),
        name="forward",
    )(*(pltpu.with_memory_space_constraint(v, pltpu.HBM) for v in (x, *consts)))


def backward_kernel(g_hbm, y_ref, r_ref, a_ref, c_ref, s_ref, o_ref, g_ref, d_ref, stage_ref, sem):
    loads = []
    for step in range(4):
        planes = (slice(None), slice(None), slice(step * 2, step * 2 + 2))
        load = pltpu.make_async_copy(g_hbm.at[planes], g_ref.at[planes], sem.at[8 + step])
        load.start()
        loads.append(load)
    for plane in range(GRP):
        if plane % 2 == 0:
            loads[plane // 2].wait()
        sides = ([], [])
        for wh in range(2):
            at = slice(wh * 8, (wh + 1) * 8)
            g = [g_ref[at, p, plane].astype(F32).reshape(64, CH) for p in range(2)]
            y = [y_ref[at, p, plane].astype(F32).reshape(64, CH) for p in range(2)]
            inv = r_ref[plane, wh : wh + 1, :]
            mean = jnp.sum(g[0] * y[0] + g[1] * y[1], axis=0, keepdims=True) * (1.0 / BAND)
            for p in range(2):
                sides[p].append((g[p] - y[p] * mean) * inv)
        for p in range(2):
            turned = jnp.concatenate(sides[p], axis=0).astype(BF16).T
            d_ref[p, :, plane * 128 : (plane + 1) * 128] = turned

    tile = 256
    tiles = SEG // 2 // tile
    copies = []
    for t in range(tiles):
        cols = slice(t * tile, (t + 1) * tile)
        pairs = band_pairs(a_ref, c_ref, s_ref, cols)
        waves = []
        for p in range(2):
            a, b = pairs[p]
            parts = []
            for plane in range(GRP):
                for band in plane_bands(plane):
                    c = c_ref[band : band + 1, cols]
                    s = s_ref[band : band + 1, cols]
                    parts.append((a * c + b * s).astype(BF16))
            waves.append(dot(d_ref[p], jnp.concatenate(parts, axis=0)))
        stage_ref[2 * t] = (waves[0] + waves[1]).astype(BF16)
        stage_ref[2 * t + 1] = (waves[0] - waves[1]).astype(BF16)
        for part in range(2):
            to = o_ref.at[:, pl.ds(part * (SEG // 2) + t * tile, tile)]
            copy = pltpu.make_async_copy(stage_ref.at[2 * t + part], to, sem.at[2 * t + part])
            copy.start()
            copies.append(copy)
    for copy in copies:
        copy.wait()


def backward(g, y, r, consts):
    return pl.pallas_call(
        backward_kernel,
        in_specs=[IN_HBM] + [IN_VMEM] * 5,
        out_specs=pl.BlockSpec(memory_space=pl.ANY),
        out_shape=jax.ShapeDtypeStruct((CH, SEG), BF16),
        scratch_shapes=[
            pltpu.VMEM((16, 2, GRP, 8, CH), BF16),
            pltpu.VMEM((2, CH, SEG // 2), BF16),
            pltpu.VMEM((8, CH, 256), BF16),
            pltpu.SemaphoreType.DMA((12,)),
        ],
        compiler_params=pltpu.CompilerParams(vmem_limit_bytes=VMEM_LIMIT),
        cost_estimate=pl.CostEstimate(flops=CH * SEG * SEG, bytes_accessed=10 << 20, transcendentals=0),
        name="backward",
    )(g, y, r, *consts)


def pack_kernel(sc_ref, re_ref, im_ref, o_ref):
    perm = regroup(True, True)
    for ri, src in enumerate((re_ref, im_ref)):
        turned = []
        for i in range(8):
            rows = []
            for ih in range(2):
                for o in range(OFFSETS):
                    val = jnp.full((CB, LANES), EMPTY, F32)
                    for s in range(SLOTS):
                        val = jnp.where(sc_ref[s] == o, src[s, ih * 8 + i], val)
                    rows.append(val)
            turned.append(jnp.concatenate(rows, axis=0).T.astype(BF16))
        for gr in range(4):
            stack = jnp.concatenate([t[gr * 32 : (gr + 1) * 32] for t in turned], axis=0)
            tile = dot(perm, stack).reshape(8, KB, 8, LANES)
            for j in range(8):
                o_ref[target_slot(sc_ref[6], gr * 8 + j), ri] = tile[j].astype(BF16)


def pack_observed(scalars, observed):
    spec = lambda base: pl.BlockSpec((SLOTS, CB, CB, LANES), lambda i, sc: (0, 0, 0, base + sc[3]))
    return pl.pallas_call(
        pack_kernel,
        grid_spec=pltpu.PrefetchScalarGridSpec(
            num_scalar_prefetch=1,
            grid=(1,),
            in_specs=[spec(0), spec(8)],
            out_specs=pl.BlockSpec((32, 2, KB, 8, LANES), lambda i, sc: (0, 0, 0, 0, 0)),
        ),
        out_shape=jax.ShapeDtypeStruct((32, 2, KB, 8, LANES), BF16),
        compiler_params=pltpu.CompilerParams(vmem_limit_bytes=VMEM_LIMIT),
        name="pack_observed",
    )(scalars, observed, observed)


def middle_kernel(sc_ref, x_ref, obs_ref, corr_ref, out_hbm, u_ref, d_ref, out_ref, sem):
    half, me = sc_ref[4], sc_ref[6]
    perm = regroup(False)
    for gr in range(8):
        y = dot(perm, x_ref[gr * 256 : (gr + 1) * 256, :]).astype(BF16)
        for r8 in range(8):
            ri, k = r8 // KB, r8 % KB
            row = ri * WINS + gr * 32
            u_ref[k, row : row + 32, :] = y[r8 * 32 : (r8 + 1) * 32]

    lane8 = lax.broadcasted_iota(jnp.int32, (8, LANES), 1)
    lane16 = lax.broadcasted_iota(jnp.int32, (16, LANES), 1)

    def correlate(k, b, width):
        cols = slice(b * LANES, (b + width) * LANES)
        lead = u_ref[k, :, b * LANES : (b + 1) * LANES]
        re_rows = u_ref[k, :WINS, cols]
        im_rows = u_ref[k, WINS:, cols]
        straight = jnp.concatenate([re_rows, im_rows], axis=0)
        crossed = jnp.concatenate([im_rows, -re_rows], axis=0)
        return dot(lead.T, jnp.concatenate([straight, crossed], axis=1))

    def weigh(k, b, width, gram):
        tiles = ([], [])
        for blk in range(8):
            a, shift = b * 8 + blk, blk * CB
            source, target = source_slot(me, a), target_slot(me, a)
            for ri in range(2):
                base = ri * width * LANES
                here = gram[shift : shift + 16, base : base + LANES]
                if shift > 0:
                    if shift > HALF and width == 2:
                        there = gram[shift : shift + 16, base + LANES : base + 2 * LANES]
                        here = jnp.where(lane16 >= shift, here, there)
                    here = pltpu.roll(here, LANES - shift, 1)
                packed = jnp.where(lane8 < HALF, here[:8], pltpu.roll(here[8:], HALF, 1))
                packed = packed * (1.0 / WINS)
                seen = obs_ref[source, ri, k].astype(F32)
                corr_ref[target, 1 - half if ri == 0 else half, k] = packed.astype(BF16)
                resid = jnp.where(seen < EMPTY / 2, packed - seen, 0.0)
                spread = jnp.concatenate([resid, pltpu.roll(resid, HALF, 1)], axis=0)
                spread = jnp.where(lane16 < HALF, spread, 0.0)
                if shift > 0:
                    spread = pltpu.roll(spread, shift, 1)
                if shift > HALF:
                    first = jnp.where(lane16 >= shift, spread, 0.0)
                    second = jnp.where(lane16 < shift, spread, 0.0)
                else:
                    first, second = spread, jnp.zeros_like(spread)
                tiles[ri].append([first, second][:width])
        res = [
            [jnp.concatenate([t[p] for t in tiles[ri]], axis=0).astype(BF16) for p in range(width)]
            for ri in range(2)
        ]
        top = jnp.concatenate([m for p in range(width) for m in (res[0][p], res[1][p])], axis=1)
        low = jnp.concatenate([m for p in range(width) for m in (-res[1][p], res[0][p])], axis=1)
        return jnp.concatenate([top, low], axis=0)

    def pull(k, b, width, weights, later):
        waves = [
            u_ref[k, ri * WINS : (ri + 1) * WINS, (b + p) * LANES : (b + p + 1) * LANES]
            for p in range(width)
            for ri in range(2)
        ]
        pushed = dot(jnp.concatenate(waves[:2], axis=1), weights)
        grad = dot(jnp.concatenate(waves, axis=1), weights, 1, 1) + pushed[:, :256]
        if b > 0:
            grad = grad + later
        d_ref[k, :WINS, b * LANES : (b + 1) * LANES] = grad[:, :LANES].astype(BF16)
        d_ref[k, WINS:, b * LANES : (b + 1) * LANES] = grad[:, LANES:].astype(BF16)
        return pushed[:, 256:]

    steps = [(k, b, 2 if b < 3 else 1) for k in range(KB) for b in range(4)]
    gram, weights, later = correlate(*steps[0]), None, None
    for i in range(len(steps) + 1):
        ahead = correlate(*steps[i + 1]) if i + 1 < len(steps) else None
        if i > 0:
            later = pull(*steps[i - 1], weights, later)
        if i < len(steps):
            weights = weigh(*steps[i], gram)
        gram = ahead
    back = regroup(True)
    copies = []
    for gr in range(8):
        rows = jnp.concatenate(
            [
                d_ref[r8 % KB, (r8 // KB) * WINS + gr * 32 : (r8 // KB) * WINS + gr * 32 + 32, :]
                for r8 in range(8)
            ],
            axis=0,
        )
        place = slice(gr * 256, (gr + 1) * 256)
        out_ref[place, :] = dot(back, rows).astype(BF16)
        copy = pltpu.make_async_copy(out_ref.at[place, :], out_hbm.at[place, :], sem.at[gr])
        copy.start()
        copies.append(copy)
    for copy in copies:
        copy.wait()


def middle(scalars, x, obs):
    return pl.pallas_call(
        middle_kernel,
        in_specs=[IN_SMEM, IN_VMEM, IN_VMEM],
        out_specs=[IN_VMEM, IN_HBM],
        scratch_shapes=[
            pltpu.VMEM((KB, 2 * WINS, CH), BF16),
            pltpu.VMEM((KB, 2 * WINS, CH), BF16),
            pltpu.VMEM((2048, CH), BF16),
            pltpu.SemaphoreType.DMA((8,)),
        ],
        out_shape=[
            jax.ShapeDtypeStruct((NB, 2, KB, 8, LANES), BF16),
            pltpu.HBM((2048, CH), BF16),
        ],
        compiler_params=pltpu.CompilerParams(vmem_limit_bytes=VMEM_LIMIT),
        name="middle",
    )(scalars, x, obs)


def unpack_kernel(sc_ref, up_ref, down_ref, o_ref):
    perm = regroup(False, True)
    low, me = sc_ref[5], sc_ref[6]
    regrouped = ([], [])
    for gr in range(4):
        sides = []
        for ref in (up_ref, down_ref):
            rows = [ref[source_slot(me, gr * 8 + j)].astype(F32).reshape(32, LANES) for j in range(8)]
            sides.append(jnp.concatenate(rows, axis=0))
        regrouped[0].append(dot(perm, jnp.where(low == 1, sides[1], sides[0]).astype(BF16)))
        regrouped[1].append(dot(perm, jnp.where(low == 1, sides[0], sides[1]).astype(BF16)))
    for h in range(2):
        for i in range(8):
            page = jnp.concatenate([r[i * 32 : (i + 1) * 32] for r in regrouped[h]], axis=0)
            turned = page.T
            for ih in range(2):
                for s in range(SLOTS):
                    val = jnp.zeros((CB, LANES), F32)
                    for o in range(OFFSETS):
                        row = ih * HALF + o * CB
                        val = jnp.where(sc_ref[s] == o, turned[row : row + CB], val)
                    o_ref[s, ih * 8 + i, :, h * LANES : (h + 1) * LANES] = val


def unpack_correl(scalars, up, down):
    block = lambda shape: pl.BlockSpec(shape, lambda i, sc: (0,) * len(shape))
    return pl.pallas_call(
        unpack_kernel,
        grid_spec=pltpu.PrefetchScalarGridSpec(
            num_scalar_prefetch=1,
            grid=(1,),
            in_specs=[block((NB, KB, 8, LANES))] * 2,
            out_specs=block((SLOTS, CB, CB, 2 * LANES)),
        ),
        out_shape=jax.ShapeDtypeStruct((SLOTS, CB, CB, 2 * LANES), F32),
        compiler_params=pltpu.CompilerParams(vmem_limit_bytes=VMEM_LIMIT),
        name="unpack_correl",
    )(scalars, up, down)


def on_device(traces, pair_lists, observed):
    consts = [jnp.asarray(v) for v in table_parts()]
    white, inverse = forward(traces[0], consts)
    white, pair_lists = lax.optimization_barrier((white, pair_lists))
    g, me = lax.axis_index("grp"), lax.axis_index("win")
    half, q = half_of(g), quarter_of(g)
    low = jnp.where(g < 4, 1, 0)
    scalars = jnp.concatenate([pair_lists[0], jnp.stack([2 * q + half, half, low, me]).astype(jnp.int32)])
    moved = lax.all_to_all(white.reshape(WINS, 8, CH), ("win", "grp"), 0, 0)
    seen = exchange(pack_observed(scalars, observed[0]))
    corr, grad = middle(scalars, moved.reshape(2048, CH), seen)
    returned = lax.all_to_all(grad.reshape(WINS, 8, CH), ("win", "grp"), 0, 0)
    corr = exchange(corr)
    up = lax.ppermute(corr[:, 0], "grp", [(i, (i + 2) % GRP) for i in range(GRP)])
    down = lax.ppermute(corr[:, 1], "grp", [(i, (i - 2) % GRP) for i in range(GRP)])
    trace_grad = backward(returned.reshape(16, 2, GRP, 8, CH), white, inverse, consts)
    up, down, trace_grad = lax.optimization_barrier((up, down, trace_grad))
    correl = unpack_correl(scalars, up, down)
    return correl[None], trace_grad[None]


def solution(mesh):
    return jax.shard_map(
        on_device,
        mesh=mesh,
        in_specs=(P(("win", "grp"), None, None), P("win", None), P("win", None, None, None, None)),
        out_specs=(P("win", None, None, None, "grp"), P(("win", "grp"), None, None)),
        check_vma=False,
    )
```
